512 devices in a mesh: frame: 16 (over x, y_lo, core), crop: 4 (over y_hi), dp: 8 (over z).
Axes of the slice: x: 4, y: 8 (y_hi: 4, y_lo: 2; y = y_hi * 2 + y_lo), z: 8, core: 2. Of those that a mesh axis runs over, the one named last changes fastest.
Arguments:
- global_clips: bfloat16 [8, 16, 256, 1408], P('dp', 'frame', 'crop'), may hold values from -6 to 6
- frame_map: int32 [8, 16, 8], P('dp', 'crop'), may hold values from 0 to 15
- teacher_qkv: bfloat16 [1408, 4224], P(None, 'frame'), may hold values from -0.15625 to 0.15625
- teacher_out: bfloat16 [1408, 1408], P('frame'), may hold values from -0.15625 to 0.15625
- teacher_bottle: bfloat16 [1408, 256], replicated, may hold values from -0.15625 to 0.15625
- student_qkv: bfloat16 [1408, 4224], P(None, 'frame'), may hold values from -0.15625 to 0.15625
- student_out: bfloat16 [1408, 1408], P('frame'), may hold values from -0.15625 to 0.15625
- student_bottle: bfloat16 [1408, 256], replicated, may hold values from -0.15625 to 0.15625
- prototypes: bfloat16 [256, 32768], P(None, 'frame'), may hold values from -1.796875 to 1.796875
- center: float32 [32768], P('frame'), may hold values from -8.6 to -3.9
Outputs:
- grad_qkv: float32 [1408, 4224], P(('crop', 'dp'), 'frame')
- grad_out: float32 [1408, 1408], P('frame', ('crop', 'dp'))
- grad_bottle: float32 [1408, 256], P(('crop', 'dp'))
The draws below stay inside these ranges and needn't reach their ends.
All inputs are finite; a program needn't handle non-finite values.
Results may differ from the reference program's by a relative error of at most 0.00035.
Values may be sent and summed in bfloat16 or wider, within the bound.
No kernel may reach another device: no remote copies, remote signals or barrier semaphores. Data moves between devices by JAX's collectives and lax.ppermute only.
A program may use at most 64 MiB of HBM per device.

```python
import math
import jax
import jax.numpy as jnp
from jax import lax

D = 1408
HEADS = 16
FRAMES = 16
PATCHES = 256
LFRAMES = 8
LOCAL_DEV = 4
BOTTLE = 256
LPATCH = 64
NTOK = 512
LOCAL_CLIPS = 16
BATCH = 8
PROTOS = 32768
N_CROP = 4


def draw_global_clips(key, part):
    first, second = jax.random.split(key, 2)
    offset = 0.8 * jax.random.normal(first, (BATCH, 1, 1, D), jnp.float32)
    values = offset + jax.random.normal(second, (BATCH, FRAMES, PATCHES, D), jnp.float32)
    return jnp.clip(values, -6.0, 6.0).astype(jnp.bfloat16)


def draw_center(key, part):
    first = jax.random.fold_in(key, 7)
    noise = jnp.clip(0.1 * jax.random.normal(first, (PROTOS,), jnp.float32), -0.3, 0.3)
    values = -4.5 + noise
    return values.astype(jnp.float32)


def plant(values, stream_key, least, high):
    index_at = [jax.random.randint(jax.random.fold_in(stream_key, axis), (), 0, length) for axis, length in enumerate(values.shape)]
    widest = values.shape.index(max(values.shape))
    next_to = index_at[:widest] + [(index_at[widest] + 1) % values.shape[widest]] + index_at[widest + 1:]
    return values.at[tuple(index_at)].set(least).at[tuple(next_to)].set(high)


def shard_levels(rng, extent, cuts, low, top_value):
    factor_of, own = 1.0, jax.random.fold_in(rng, 6)
    for position, blocks in cuts:
        draws = jnp.exp(jax.random.uniform(jax.random.fold_in(own, position), (blocks,), jnp.float32, low / len(cuts), top_value / len(cuts)))
        factor_of = factor_of * jnp.repeat(draws, extent[position] // blocks).reshape([-1 if axis == position else 1 for axis in range(len(extent))])
    return factor_of


def normal_values(rng, shape, width, limit, pieces=(), held_as=jnp.bfloat16):
    entries = width * jax.random.normal(rng, shape, jnp.float32)
    if pieces:
        entries = entries * shard_levels(rng, shape, pieces, -0.22, 0.18)
    return jnp.clip(entries, -limit, limit).astype(held_as)


def setup_inputs(seed: int = 0) -> dict:
    splits = jax.random.split(jax.random.key(seed), 11)
    return {
        "global_clips": draw_global_clips(jax.random.fold_in(splits[10], 71), 0),
        "frame_map": plant(jax.random.randint(splits[1], (BATCH, LOCAL_CLIPS, LFRAMES), 0, FRAMES), jax.random.fold_in(splits[1], 1), 0, FRAMES - 1).astype(jnp.int32),
        "teacher_qkv": normal_values(splits[2], (D, 3 * D), D ** -0.5, 0.15625, ((1, 16),)),
        "teacher_out": normal_values(splits[3], (D, D), D ** -0.5, 0.15625, ((0, 16),)),
        "teacher_bottle": normal_values(splits[4], (D, BOTTLE), D ** -0.5, 0.15625),
        "student_qkv": normal_values(splits[5], (D, 3 * D), D ** -0.5, 0.15625, ((1, 16),)),
        "student_out": normal_values(splits[6], (D, D), D ** -0.5, 0.15625, ((0, 16),)),
        "student_bottle": normal_values(splits[7], (D, BOTTLE), D ** -0.5, 0.15625),
        "prototypes": normal_values(splits[8], (BOTTLE, PROTOS), 0.3, 1.796875, ((1, 16),)),
        "center": draw_center(jax.random.fold_in(splits[10], 71), 0),
    }


HIGH = lax.Precision.HIGHEST
TAU_TEACH = 0.04
TAU_STUD = 0.1

def norm_tokens(tokens):
    values = tokens.astype(jnp.float32)
    middle = lax.optimization_barrier(jnp.mean(values, axis=-1, keepdims=True))
    spread = lax.optimization_barrier(jnp.mean(jnp.square(values - middle), axis=-1, keepdims=True))
    return ((values - middle) * lax.rsqrt(spread + 1e-06)).astype(jnp.bfloat16)

def attend_core(qkv):
    rounded = lax.optimization_barrier(qkv.astype(jnp.bfloat16)).astype(jnp.float32)
    query = rounded[:, :, :, 0]
    keys = rounded[:, :, :, 1]
    values = rounded[:, :, :, 2]
    scale = 1.0 / math.sqrt(qkv.shape[-1])
    scores = jnp.einsum('iphe,jphe->phij', query, keys, precision=HIGH) * scale
    weights = jax.nn.softmax(scores, axis=-1)
    weights = lax.optimization_barrier(weights.astype(jnp.bfloat16)).astype(jnp.float32)
    return jnp.einsum('phij,jphe->iphe', weights, values, precision=HIGH)

def project(normed, weight32):
    qkv = jnp.einsum('fpd,dc->fpc', normed.astype(jnp.float32), weight32, precision=HIGH)
    return qkv.reshape(normed.shape[0], normed.shape[1], HEADS, 3, -1)

def unit(vector):
    return vector * lax.rsqrt(lax.optimization_barrier(jnp.sum(vector * vector, axis=-1, keepdims=True)) + 1e-06)

def reference(global_clips, frame_map, teacher_qkv, teacher_out, teacher_bottle, student_qkv, student_out, student_bottle, prototypes, center):
    protos = prototypes.astype(jnp.float32)
    t_qkv = teacher_qkv.astype(jnp.float32)
    t_out = teacher_out.astype(jnp.float32)
    t_bottle = teacher_bottle.astype(jnp.float32)
    s_qkv = student_qkv.astype(jnp.float32)
    s_out = student_out.astype(jnp.float32)
    s_bottle = student_bottle.astype(jnp.float32)
    crop_of = jnp.arange(LOCAL_CLIPS, dtype=jnp.int32) // LOCAL_DEV

    def one_clip(index):
        clip = lax.dynamic_index_in_dim(global_clips, index, 0, keepdims=False)
        maps = lax.dynamic_index_in_dim(frame_map, index, 0, keepdims=False)
        normed = norm_tokens(clip)
        t_att = attend_core(project(normed, t_qkv))
        t_mean = lax.optimization_barrier(jnp.sum(t_att, axis=(0, 1))).reshape(-1) / (FRAMES * PATCHES)
        pooled_t = lax.optimization_barrier(jnp.mean(clip.astype(jnp.float32), axis=(0, 1))) + jnp.dot(t_mean, t_out, precision=HIGH)
        unit_t = unit(jnp.dot(pooled_t, t_bottle, precision=HIGH))
        probs = jax.nn.softmax((jnp.dot(unit_t, protos, precision=HIGH) - center) / TAU_TEACH)
        crops = clip.reshape(FRAMES, N_CROP, LPATCH, D)
        local = crops[maps.T, crop_of[None, :]]
        local_mean = lax.optimization_barrier(jnp.mean(local.astype(jnp.float32), axis=(0, 2)))
        local_normed = norm_tokens(local).reshape(LFRAMES, LOCAL_CLIPS * LPATCH, D)

        def loss_fn(w_qkv, w_out, w_bottle):
            s_att = attend_core(project(local_normed, w_qkv))
            s_mean = lax.optimization_barrier(jnp.sum(s_att.reshape(LFRAMES, LOCAL_CLIPS, LPATCH, D), axis=(0, 2))) / NTOK
            pooled_s = local_mean + jnp.dot(s_mean, w_out, precision=HIGH)
            unit_s = unit(jnp.dot(pooled_s, w_bottle, precision=HIGH))
            log_q = jax.nn.log_softmax(jnp.dot(unit_s, protos, precision=HIGH) / TAU_STUD, axis=-1)
            return -jnp.sum(log_q * probs[None, :]) / LOCAL_CLIPS
        return jax.grad(loss_fn, argnums=(0, 1, 2))(s_qkv, s_out, s_bottle)
    grads = lax.map(one_clip, jnp.arange(BATCH, dtype=jnp.int32))
    return (lax.optimization_barrier(jnp.sum(grads[0], axis=0)), lax.optimization_barrier(jnp.sum(grads[1], axis=0)), lax.optimization_barrier(jnp.sum(grads[2], axis=0)))
```

```python
import functools
import math

import jax
import jax.numpy as jnp
from jax import lax
from jax.experimental import pallas as pl
from jax.experimental.pallas import tpu as pltpu
from jax.sharding import PartitionSpec as P

D = 1408
HEADS = 16
HS = 88
FRAMES = 16
BOTTLE = 256
GP = 16
ROWS = FRAMES * GP
CLIPS = 4
NTOK = 512
NTEACH = 4096
TAU_TEACH = 0.04
TAU_STUD = 0.1
ALL_CLIPS = 16
HIGH = lax.Precision.HIGHEST
F32 = jnp.float32
BF16 = jnp.bfloat16
NEG = -1e30
SCALE = 1.0 / math.sqrt(HS)
MSG = 24
QROWS = 56
STEP = 64.0
INTERPRET = False

NN = (((1,), (0,)), ((), ()))
NT = (((1,), (1,)), ((), ()))
TN = (((0,), (0,)), ((), ()))


def call(kernel, outs, *args, scratch=(), smem=0):
    spec = [pl.BlockSpec(memory_space=pltpu.SMEM)] * smem
    spec += [pl.BlockSpec(memory_space=pltpu.VMEM)] * (len(args) - smem)
    return pl.pallas_call(
        kernel,
        out_shape=tuple(jax.ShapeDtypeStruct(shape, dtype) for shape, dtype in outs),
        in_specs=spec,
        out_specs=tuple(pl.BlockSpec(memory_space=pltpu.VMEM) for _ in outs),
        scratch_shapes=list(scratch),
        interpret=INTERPRET,
    )(*args)


def mm(a, b, dims=NN):
    return lax.dot_general(a, b, dims, preferred_element_type=F32)


def mmh(a, b, dims=NN):
    return lax.dot_general(a, b, dims, precision=HIGH, preferred_element_type=F32)


def pieces(x):
    top = x.astype(BF16)
    rest = x - top.astype(F32)
    mid = rest.astype(BF16)
    return top, mid, (rest - mid.astype(F32)).astype(BF16)


def mm3(x, y, dims=NN):
    top, mid, low = pieces(x)
    return mm(top, y, dims) + (mm(mid, y, dims) + mm(low, y, dims))


def rsqrt(x):
    guess = lax.rsqrt(x)
    return guess * (1.5 - 0.5 * x * guess * guess)


def same_patch():
    row = lax.broadcasted_iota(jnp.int32, (ROWS, ROWS), 0)
    col = lax.broadcasted_iota(jnp.int32, (ROWS, ROWS), 1)
    return jnp.where((row % GP) == (col % GP), 0.0, NEG).astype(F32)


def split_qkv(flat):
    rounded = flat.astype(BF16)
    return rounded[:, :HS], rounded[:, HS : 2 * HS], rounded[:, 2 * HS :]


def prep_kernel(tok, t_out, t_oth, s_out, s_oth, t_bot, s_bot, mt, ms, osum, otz, osz):
    total = jnp.sum(tok[...].astype(F32), axis=0, keepdims=True)
    osum[...] = total
    otz[...] = mm3(total, t_bot[...])
    osz[...] = mm3(total, s_bot[...])
    mt[0] = mm(t_out[...], t_bot[...])
    mt[1] = mm(t_oth[...], t_bot[...])
    ms[0] = mm(s_out[...], s_bot[...])
    ms[1] = mm(s_oth[...], s_bot[...])


def teacher_kernel(x, w_own, w_oth, mt, otz, normed, zt):
    mask = same_patch()
    sums = [jnp.zeros((1, HS), F32), jnp.zeros((1, HS), F32)]
    for group in range(2):
        values = x[:, group * GP : (group + 1) * GP, :].reshape(ROWS, D).astype(F32)
        middle = jnp.mean(values, axis=-1, keepdims=True)
        moved = values - middle
        spread = jnp.mean(moved * moved, axis=-1, keepdims=True)
        token = (moved * rsqrt(spread + 1e-06)).astype(BF16)
        normed[group] = token
        for head, weight in enumerate((w_own, w_oth)):
            query, key, value = split_qkv(mm(token, weight[...]))
            scores = mm(query, key, NT) * SCALE + mask
            scores = jnp.exp(scores - jnp.max(scores, axis=-1, keepdims=True))
            share = scores / jnp.sum(scores, axis=-1, keepdims=True)
            att = mm(share.astype(BF16), value)
            sums[head] = sums[head] + jnp.sum(att, axis=0, keepdims=True)
    zt[...] = (mmh(sums[0], mt[0]) + mmh(sums[1], mt[1]) + otz[...]) / NTEACH


def student_kernel(normed, w_own, w_oth, ms, s_out, s_oth, osum, osz, ccol, crow, cown, own, oth, zs, pooled, heads):
    mask = same_patch()
    sums = [jnp.zeros((CLIPS, HS), F32), jnp.zeros((CLIPS, HS), F32)]
    for group in range(2):
        token = normed[group]
        for head, (weight, keep) in enumerate(((w_own, own), (w_oth, oth))):
            query, key, value = split_qkv(mm(token, weight[...]))
            keep[0, group] = query
            keep[1, group] = key
            keep[2, group] = value
            scores = mm(query, key, NT) * SCALE + mask
            totals = []
            for clip in range(CLIPS):
                count = ccol[clip : clip + 1, :]
                here = jnp.where(count > 0.0, scores, NEG)
                here = jnp.exp(here - jnp.max(here, axis=-1, keepdims=True))
                share = here / jnp.sum(here * count, axis=-1, keepdims=True)
                share = share.astype(BF16).astype(F32) * crow[:, clip : clip + 1]
                totals.append(jnp.sum(share, axis=0, keepdims=True) * count)
            sums[head] = sums[head] + mm3(jnp.concatenate(totals, axis=0), value)
    share_own = sums[0] / NTOK
    share_oth = sums[1] / NTOK
    heads[0] = share_own
    heads[1] = share_oth
    frac = cown[...] / NTOK
    zs[...] = mmh(share_own, ms[0]) + mmh(share_oth, ms[1]) + frac * osz[...]
    pooled[...] = mm3(share_own, s_out[...]) + mm3(share_oth, s_oth[...]) + frac * osum[...]


def message_kernel(frame, zs, ztc, pooled, heads, out):
    me = frame[0]
    zt = jnp.sum(ztc[...], axis=0)
    for peer in range(FRAMES):
        out[peer, 0:4, :] = zs[:, 0:128]
        out[peer, 4:8, :] = zs[:, 128:256]
        out[peer, 8:9, :] = zt[:, 0:128]
        out[peer, 9:10, :] = zt[:, 128:256]
        out[peer, 10:MSG, :] = jnp.zeros((MSG - 10, 128), F32)
        out[peer, 10:14, 0:HS] = pooled[:, peer * HS : (peer + 1) * HS]
        mine = (me == peer).astype(F32)
        partner = (jnp.bitwise_xor(me, 1) == peer).astype(F32)
        out[peer, 14:18, 0:HS] = heads[0] * mine + heads[1] * partner


def logits_kernel(got, protos, center, out, zs, heads):
    total = got[0]
    for source in range(1, FRAMES):
        total = total + got[source]
    z_s = jnp.concatenate([total[0:4], total[4:8]], axis=1)
    z_t = jnp.concatenate([total[8:9], total[9:10]], axis=1)
    zs[...] = z_s
    heads[...] = total[14:18, 0:HS]
    z_all = jnp.concatenate([z_s, z_t], axis=0)
    unit = z_all * rsqrt(jnp.sum(z_all * z_all, axis=-1, keepdims=True) + 1e-06)
    wide = mm3(unit, protos[...])
    logits = jnp.concatenate([wide[0:4] / TAU_STUD, (wide[4:5] - center[...]) / TAU_TEACH], axis=0)
    top = jnp.max(logits, axis=-1, keepdims=True)
    grown = jnp.exp(logits - top)
    size = jnp.sum(grown, axis=-1, keepdims=True)
    vec = mm3(grown, protos[...], NT)
    lane = lax.broadcasted_iota(jnp.int32, (5, 128), 1)
    tops = jnp.where(lane == 0, top, jnp.where(lane == 1, size, 0.0))
    for peer in range(FRAMES):
        out[peer, 0:5, :] = vec[:, 0:128]
        out[peer, 5:10, :] = vec[:, 128:256]
        out[peer, 10:15, :] = tops
        out[peer, 15:19, :] = total[10:14]
        out[peer, 19:MSG, :] = jnp.zeros((MSG - 19, 128), F32)


def code_of(peak):
    return jnp.ceil(jnp.log(jnp.maximum(peak, 1e-30)) * (STEP / math.log(2.0))) + 1.0


def scale_of(code):
    return jnp.exp(code * (math.log(2.0) / STEP))


def whole_max(x):
    return jnp.max(jnp.max(x, axis=-1, keepdims=True), axis=0, keepdims=True)


def back_kernel(peers, got, zs, heads, ms, normed, normed_oth, own, oth, ccol, crow, out, grad, last, line):
    tops = [got[source, 10:15, 0:1] for source in range(FRAMES)]
    top = functools.reduce(jnp.maximum, tops)
    size = jnp.zeros((5, 1), F32)
    low = jnp.zeros((5, 128), F32)
    high = jnp.zeros((5, 128), F32)
    for source in range(FRAMES):
        factor = jnp.exp(tops[source] - top)
        size = size + got[source, 10:15, 1:2] * factor
        low = low + got[source, 0:5, :] * factor
        high = high + got[source, 5:10, :] * factor
    expect = jnp.concatenate([low, high], axis=1) / size
    d_unit = (expect[0:4] - expect[4:5]) / (ALL_CLIPS * TAU_STUD)
    z_s = zs[...]
    inverse = rsqrt(jnp.sum(z_s * z_s, axis=-1, keepdims=True) + 1e-06)
    unit = z_s * inverse
    d_z = (d_unit - unit * jnp.sum(unit * d_unit, axis=-1, keepdims=True)) * inverse
    d_heads = mmh(d_z, ms[0], NT) / NTOK
    mask = same_patch()
    packed = []
    for half, keep in ((0, own), (1, oth)):
        for group in range(2):
            query, key, value = (keep[part, group] for part in range(3))
            scores = mm(query, key, NT) * SCALE + mask
            d_weights = mm3(d_heads, value, NT).astype(BF16).astype(F32)
            total_q = jnp.zeros((ROWS, HS), F32)
            total_k = jnp.zeros((ROWS, HS), F32)
            total_v = jnp.zeros((ROWS, HS), F32)
            for clip in range(CLIPS):
                count = ccol[clip : clip + 1, :]
                many = crow[:, clip : clip + 1]
                here = jnp.where(count > 0.0, scores, NEG)
                here = jnp.exp(here - jnp.max(here, axis=-1, keepdims=True))
                share = here / jnp.sum(here * count, axis=-1, keepdims=True)
                d_w = d_weights[clip : clip + 1, :]
                inner = jnp.sum(share * count * d_w, axis=-1, keepdims=True)
                d_s = share * (d_w - inner) * SCALE
                d_q = mm3(d_s * count, key)
                d_k = mm3(d_s * many, query, TN)
                received = jnp.sum(share.astype(BF16).astype(F32) * many, axis=0, keepdims=True)
                d_v = mmh(received, d_heads[clip : clip + 1, :], TN)
                total_q = total_q + many * d_q.astype(BF16).astype(F32)
                total_k = total_k + many * d_k.astype(BF16).astype(F32)
                total_v = total_v + many * d_v.astype(BF16).astype(F32)
            packed.append(jnp.concatenate([total_q, total_k, total_v], axis=1))
    for index in range(4):
        token = normed[index] if index < 2 else normed_oth[index - 2]
        first = packed[index].astype(BF16)
        second = (packed[index] - first.astype(F32)).astype(BF16)
        wide = mm(token, first, TN) + mm(token, second, TN)
        if index == 0:
            grad[...] = wide
        else:
            grad[...] += wide
    full = grad[...]
    main = full[:, 0:256]
    code = code_of(jnp.max(jnp.abs(main), axis=0, keepdims=True))
    grad[:, 0:256] = jnp.round(main * (32000.0 / scale_of(code)))
    thin = jnp.transpose(full[:, 256:264])
    code_thin = code_of(jnp.max(jnp.abs(thin), axis=-1, keepdims=True))
    last[...] = jnp.round(thin * (32000.0 / scale_of(code_thin)))
    code_z = code_of(whole_max(jnp.abs(d_z)))
    sent_z = jnp.round(d_z * (32000.0 / scale_of(code_z)))
    mine = heads[...]
    code_h = code_of(whole_max(jnp.abs(mine)))
    sent_h = jnp.round(mine * (32000.0 / scale_of(code_h)))
    pooled = jnp.concatenate([got[source, 15:19, 0:HS] for source in range(FRAMES)], axis=1)
    code_p = code_of(whole_max(jnp.abs(pooled)))
    sent_p = jnp.round(pooled * (32000.0 / scale_of(code_p)))
    lane = lax.broadcasted_iota(jnp.int32, (1, 128), 1)
    codes = jnp.where(lane == 64, code_z, jnp.where(lane == 65, code_h, jnp.where(lane == 66, code_p, 0.0)))
    block = D // peers
    line[...] = jnp.zeros((QROWS, 256), F32)
    line[44:48, :] = sent_z
    line[48:49, 0:HS] = sent_h[0:1]
    line[48:49, 128 : 128 + HS] = sent_h[1:2]
    line[49:50, 0:HS] = sent_h[2:3]
    line[49:50, 128 : 128 + HS] = sent_h[3:4]
    line[55:56, :] = code
    for peer in range(peers):
        line[0:block, :] = grad[peer * block : (peer + 1) * block, 0:256]
        part = sent_p[:, peer * block : (peer + 1) * block]
        line[50:54, 0:block] = part
        thin_part = last[:, peer * block : (peer + 1) * block]
        line[50:54, 64 : 64 + block] = thin_part[0:4]
        line[50:54, 128 : 128 + block] = thin_part[4:8]
        line[50:54, 192:193] = code_thin[0:4]
        line[50:54, 193:194] = code_thin[4:8]
        line[54:55, 0:128] = codes
        out[peer] = line[...].astype(jnp.int32).astype(jnp.int16)


def final_kernel(peers, got, bottle, g_qkv, g_out, g_bottle, z_all, h_all, p_all):
    block = D // peers
    main = jnp.zeros((block, 256), F32)
    thin_a = jnp.zeros((4, block), F32)
    thin_b = jnp.zeros((4, block), F32)
    for source in range(peers):
        line = got[source].astype(jnp.int32).astype(F32)
        main = main + line[0:block] * (scale_of(line[55:56]) / 32000.0)
        thin_a = thin_a + line[50:54, 64 : 64 + block] * (scale_of(line[50:54, 192:193]) / 32000.0)
        thin_b = thin_b + line[50:54, 128 : 128 + block] * (scale_of(line[50:54, 193:194]) / 32000.0)
        scales = scale_of(line[54:55, 0:128]) / 32000.0
        first = source * CLIPS
        z_all[first : first + 4, :] = line[44:48] * scales[:, 64:65]
        scale_h = scales[:, 65:66]
        h_all[first : first + 1, :] = line[48:49, 0:HS] * scale_h
        h_all[first + 1 : first + 2, :] = line[48:49, 128 : 128 + HS] * scale_h
        h_all[first + 2 : first + 3, :] = line[49:50, 0:HS] * scale_h
        h_all[first + 3 : first + 4, :] = line[49:50, 128 : 128 + HS] * scale_h
        p_all[first : first + 4, :] = line[50:54, 0:block] * scales[:, 66:67]
    g_qkv[:, 0:256] = main
    g_qkv[:, 256:264] = jnp.transpose(jnp.concatenate([thin_a, thin_b], axis=0))
    d_z = z_all[...]
    g_bottle[...] = mmh(p_all[...], d_z, TN)
    g_out[...] = mmh(mmh(h_all[...], d_z, TN), bottle[...].astype(F32), NT)


def local(
    global_clips,
    frame_map,
    teacher_qkv,
    teacher_out,
    teacher_bottle,
    student_qkv,
    student_out,
    student_bottle,
    prototypes,
    center,
):
    frame = lax.axis_index("frame")
    peers = lax.axis_size("crop") * lax.axis_size("dp")
    crops = lax.axis_size("crop")
    swap = [(index, index ^ 1) for index in range(FRAMES)]
    tokens = global_clips[0, 0]
    halves = jnp.broadcast_to(tokens.reshape(1, 2, 32, D), (FRAMES // 2, 2, 32, D)).reshape(FRAMES, 32, D)
    mixed = lax.all_to_all(halves, "frame", 0, 0, tiled=True)
    t_oth = lax.ppermute(teacher_qkv, "frame", swap)
    s_oth = lax.ppermute(student_qkv, "frame", swap)
    outs_oth = lax.ppermute(jnp.stack([teacher_out, student_out]), "frame", swap)
    maps = frame_map[0]
    counts = jnp.sum((maps[:, :, None] == jnp.arange(FRAMES, dtype=jnp.int32)[None, None, :]).astype(F32), axis=1)
    ccol = jnp.repeat(counts, GP, axis=1)
    crow = ccol.T
    cown = jnp.sum((maps == frame).astype(F32), axis=1, keepdims=True)
    mt, ms, osum, otz, osz = call(
        prep_kernel,
        [((2, HS, BOTTLE), F32), ((2, HS, BOTTLE), F32), ((1, D), F32), ((1, BOTTLE), F32), ((1, BOTTLE), F32)],
        tokens, teacher_out, outs_oth[0], student_out, outs_oth[1], teacher_bottle, student_bottle,
    )
    normed, zt = call(
        teacher_kernel,
        [((2, ROWS, D), BF16), ((1, BOTTLE), F32)],
        mixed, teacher_qkv, t_oth, mt, otz,
    )
    ztc = lax.all_to_all(jnp.broadcast_to(zt[None], (crops, 1, BOTTLE)), "crop", 0, 0, tiled=True)
    own, oth, zs, pooled, heads = call(
        student_kernel,
        [
            ((3, 2, ROWS, HS), BF16),
            ((3, 2, ROWS, HS), BF16),
            ((CLIPS, BOTTLE), F32),
            ((CLIPS, D), F32),
            ((2, CLIPS, HS), F32),
        ],
        normed, student_qkv, s_oth, ms, student_out, outs_oth[1], osum, osz, ccol, crow, cown,
    )
    normed_oth = lax.ppermute(normed, "frame", swap)
    kept_oth = lax.ppermute(oth, "frame", swap)
    (sent,) = call(
        message_kernel,
        [((FRAMES, MSG, 128), F32)],
        frame.astype(jnp.int32).reshape(1), zs, ztc, pooled, heads, smem=1,
    )
    got = lax.all_to_all(sent, "frame", 0, 0, tiled=True)
    sent, z_s, my_heads = call(
        logits_kernel,
        [((FRAMES, MSG, 128), F32), ((CLIPS, BOTTLE), F32), ((CLIPS, HS), F32)],
        got, prototypes, center.reshape(1, -1),
    )
    got = lax.all_to_all(sent, "frame", 0, 0, tiled=True)
    (sent,) = call(
        functools.partial(back_kernel, peers),
        [((peers, QROWS, 256), jnp.int16)],
        got, z_s, my_heads, ms, normed, normed_oth, own, kept_oth, ccol, crow,
        scratch=[pltpu.VMEM((D, 3 * HS), F32), pltpu.VMEM((8, D), F32), pltpu.VMEM((QROWS, 256), F32)],
    )
    got = lax.all_to_all(sent, ("crop", "dp"), 0, 0, tiled=True)
    block = D // peers
    place = lax.axis_index("crop") * lax.axis_size("dp") + lax.axis_index("dp")
    bottle = lax.dynamic_slice_in_dim(student_bottle, place * block, block, axis=0)
    return call(
        functools.partial(final_kernel, peers),
        [((block, 3 * HS), F32), ((HS, block), F32), ((block, BOTTLE), F32)],
        got, bottle,
        scratch=[
            pltpu.VMEM((peers * CLIPS, BOTTLE), F32),
            pltpu.VMEM((peers * CLIPS, HS), F32),
            pltpu.VMEM((peers * CLIPS, block), F32),
        ],
    )


def solution(mesh):
    return jax.shard_map(
        local,
        mesh=mesh,
        in_specs=(
            P("dp", "frame", "crop", None),
            P("dp", "crop", None),
            P(None, "frame"),
            P("frame", None),
            P(),
            P(None, "frame"),
            P("frame", None),
            P(),
            P(None, "frame"),
            P("frame"),
        ),
        out_specs=(P(("crop", "dp"), "frame"), P("frame", ("crop", "dp")), P(("crop", "dp"), None)),
        check_vma=False,
    )
```

```python
import functools
import math

import jax
import jax.numpy as jnp
from jax import lax
from jax.experimental import pallas as pl
from jax.experimental.pallas import tpu as pltpu
from jax.sharding import PartitionSpec as P

D = 1408
HEADS = 16
HS = 88
FRAMES = 16
BOTTLE = 256
GP = 8
ROWS = FRAMES * GP
TILES = 4
LFRAMES = 8
CLIPS = 4
NTOK = 512
NTEACH = 4096
TAU_TEACH = 0.04
TAU_STUD = 0.1
ALL_CLIPS = 16
HIGH = lax.Precision.HIGHEST
F32 = jnp.float32
BF16 = jnp.bfloat16
NEG = -1e30
SCALE = 1.0 / math.sqrt(HS)
MSG = 24
QROWS = 56
STEP = 64.0
INTERPRET = False

NN = (((1,), (0,)), ((), ()))
NT = (((1,), (1,)), ((), ()))
TN = (((0,), (0,)), ((), ()))


def call(kernel, outs, *args, scratch=(), smem=0, limit=16):
    spec = [pl.BlockSpec(memory_space=pltpu.SMEM)] * smem
    spec += [pl.BlockSpec(memory_space=pltpu.VMEM)] * (len(args) - smem)
    return pl.pallas_call(
        kernel,
        out_shape=tuple(jax.ShapeDtypeStruct(shape, dtype) for shape, dtype in outs),
        in_specs=spec,
        out_specs=tuple(pl.BlockSpec(memory_space=pltpu.VMEM) for _ in outs),
        scratch_shapes=list(scratch),
        compiler_params=pltpu.CompilerParams(vmem_limit_bytes=limit * 2**20),
        interpret=INTERPRET,
    )(*args)


def mm(a, b, dims=NN):
    return lax.dot_general(a, b, dims, preferred_element_type=F32)


def mmh(a, b, dims=NN):
    return lax.dot_general(a, b, dims, precision=HIGH, preferred_element_type=F32)


def pieces(x):
    top = x.astype(BF16)
    rest = x - top.astype(F32)
    mid = rest.astype(BF16)
    return top, mid, (rest - mid.astype(F32)).astype(BF16)


def mm3(x, y, dims=NN):
    top, mid, low = pieces(x)
    return mm(top, y, dims) + (mm(mid, y, dims) + mm(low, y, dims))


def rsqrt(x):
    guess = lax.rsqrt(x)
    return guess * (1.5 - 0.5 * x * guess * guess)


def same_patch():
    row = lax.broadcasted_iota(jnp.int32, (ROWS, ROWS), 0)
    col = lax.broadcasted_iota(jnp.int32, (ROWS, ROWS), 1)
    return jnp.where((row % GP) == (col % GP), 0.0, NEG).astype(F32)


def split_qkv(flat):
    rounded = flat.astype(BF16)
    return rounded[:, :HS], rounded[:, HS : 2 * HS], rounded[:, 2 * HS :]


def prep_kernel(
    maps, frame, tok, t_out, t_oth, s_out, s_oth, t_bot, s_bot, mt, ms, otz, zlocal, plocal, ccol, crow
):
    total = jnp.sum(tok[...].astype(F32), axis=0, keepdims=True)
    otz[...] = mm3(total, t_bot[...])
    osz = mm3(total, s_bot[...])
    mt[0] = mm(t_out[...], t_bot[...])
    mt[1] = mm(t_oth[...], t_bot[...])
    ms[0] = mm(s_out[...], s_bot[...])
    ms[1] = mm(s_oth[...], s_bot[...])
    lane = lax.broadcasted_iota(jnp.int32, (1, ROWS), 1)
    row = lax.broadcasted_iota(jnp.int32, (ROWS, ROWS), 0) // GP
    down = jnp.zeros((ROWS, ROWS), F32)
    across = [jnp.zeros((1, ROWS), F32) for _ in range(CLIPS)]
    mine = [jnp.zeros((1, ROWS), F32) for _ in range(CLIPS)]
    for step in range(LFRAMES):
        shown = jnp.full((1, ROWS), -1, jnp.int32)
        for clip in range(CLIPS):
            index = maps[clip, step]
            shown = jnp.where(lane == clip, index, shown)
            across[clip] = across[clip] + jnp.where(lane // GP == index, 1.0, 0.0)
            mine[clip] = mine[clip] + jnp.where(index == frame[0], 1.0, 0.0)
        down = down + jnp.where(row == shown, 1.0, 0.0)
    crow[...] = down
    for clip in range(CLIPS):
        ccol[clip : clip + 1, :] = across[clip]
        frac = mine[clip][:, 0:1] / NTOK
        zlocal[clip : clip + 1, :] = frac * osz
        plocal[clip : clip + 1, :] = frac * total


def teacher_kernel(x, w_own, w_oth, mt, otz, normed, zt):
    for group in range(2):
        values = x[:, group * 2 * GP : (group + 1) * 2 * GP, :].astype(F32)
        middle = jnp.mean(values, axis=-1, keepdims=True)
        moved = values - middle
        spread = jnp.mean(moved * moved, axis=-1, keepdims=True)
        token = moved * rsqrt(spread + 1e-06)
        normed[2 * group] = token[:, :GP].reshape(ROWS, D).astype(BF16)
        normed[2 * group + 1] = token[:, GP:].reshape(ROWS, D).astype(BF16)
    mask = same_patch()
    tokens = normed[...].reshape(TILES * ROWS, D)
    total = otz[...]
    for head, weight in enumerate((w_own, w_oth)):
        flat = mm(tokens, weight[...], NT)
        summed = jnp.zeros((1, HS), F32)
        for tile in range(TILES):
            query, key, value = split_qkv(flat[tile * ROWS : (tile + 1) * ROWS])
            scores = mm(query, key, NT) * SCALE + mask
            scores = jnp.exp(scores - jnp.max(scores, axis=-1, keepdims=True))
            share = scores / jnp.sum(scores, axis=-1, keepdims=True)
            att = mm(share.astype(BF16), value)
            summed = summed + jnp.sum(att, axis=0, keepdims=True)
        total = total + mmh(summed, mt[head])
    for crop in range(zt.shape[0]):
        zt[crop] = total / NTEACH


def clip_shares(scores, count):
    here = jnp.where(count > 0.0, scores, NEG)
    here = jnp.exp(here - jnp.max(here, axis=-1, keepdims=True))
    return here / jnp.sum(here * count, axis=-1, keepdims=True)


def student_kernel(normed, w_own, w_oth, ms, s_out, s_oth, zlocal, plocal, ccol, crow, own, oth, zs, pooled, heads):
    mask = same_patch()
    tokens = normed[...].reshape(TILES * ROWS, D)
    for head, (weight, keep) in enumerate(((w_own, own), (w_oth, oth))):
        flat = mm(tokens, weight[...], NT)
        summed = jnp.zeros((CLIPS, HS), F32)
        for tile in range(TILES):
            query, key, value = split_qkv(flat[tile * ROWS : (tile + 1) * ROWS])
            keep[0, tile] = query
            keep[1, tile] = key
            keep[2, tile] = value
            scores = mm(query, key, NT) * SCALE + mask
            totals = []
            for clip in range(CLIPS):
                count = ccol[clip : clip + 1, :]
                share = clip_shares(scores, count).astype(BF16).astype(F32) * crow[:, clip : clip + 1]
                totals.append(jnp.sum(share, axis=0, keepdims=True) * count)
            summed = summed + mm3(jnp.concatenate(totals, axis=0), value)
        heads[head] = summed / NTOK
    zs[...] = mmh(heads[0], ms[0]) + mmh(heads[1], ms[1]) + zlocal[...]
    pooled[...] = mm3(heads[0], s_out[...]) + mm3(heads[1], s_oth[...]) + plocal[...]


def shares_kernel(keep, ccol, crow, by_query, by_key, received):
    mask = same_patch()
    lane = lax.broadcasted_iota(jnp.int32, (ROWS, ROWS), 1)
    for tile in range(TILES):
        scores = mm(keep[0, tile], keep[1, tile], NT) * SCALE + mask
        taken = jnp.zeros((ROWS, ROWS), F32)
        for clip in range(CLIPS):
            count = ccol[clip : clip + 1, :]
            share = clip_shares(scores, count)
            by_query[tile, clip] = share * count
            flipped = jnp.transpose(share)
            by_key[tile, clip] = flipped * count
            part = jnp.sum(flipped.astype(BF16).astype(F32) * count, axis=-1, keepdims=True)
            taken = jnp.where(lane == clip, part, taken)
        received[tile] = taken


def flip_kernel(normed, out):
    out[...] = jnp.transpose(normed[...].reshape(TILES * ROWS, D))


def message_kernel(frame, zs, ztc, pooled, heads, out):
    me = frame[0]
    zt = jnp.sum(ztc[...], axis=0)
    for peer in range(FRAMES):
        out[peer, 0:4, :] = zs[:, 0:128]
        out[peer, 4:8, :] = zs[:, 128:256]
        out[peer, 8:9, :] = zt[:, 0:128]
        out[peer, 9:10, :] = zt[:, 128:256]
        out[peer, 10:MSG, :] = jnp.zeros((MSG - 10, 128), F32)
        out[peer, 10:14, 0:HS] = pooled[:, peer * HS : (peer + 1) * HS]
        mine = (me == peer).astype(F32)
        partner = (jnp.bitwise_xor(me, 1) == peer).astype(F32)
        out[peer, 14:18, 0:HS] = heads[0] * mine + heads[1] * partner


def logits_kernel(got, protos, center, out, zs, heads):
    total = got[0]
    for source in range(1, FRAMES):
        total = total + got[source]
    z_s = jnp.concatenate([total[0:4], total[4:8]], axis=1)
    z_t = jnp.concatenate([total[8:9], total[9:10]], axis=1)
    zs[...] = z_s
    heads[...] = total[14:18, 0:HS]
    z_all = jnp.concatenate([z_s, z_t], axis=0)
    unit = z_all * rsqrt(jnp.sum(z_all * z_all, axis=-1, keepdims=True) + 1e-06)
    wide = mm3(unit, protos[...])
    logits = jnp.concatenate([wide[0:4] / TAU_STUD, (wide[4:5] - center[...]) / TAU_TEACH], axis=0)
    top = jnp.max(logits, axis=-1, keepdims=True)
    grown = jnp.exp(logits - top)
    size = jnp.sum(grown, axis=-1, keepdims=True)
    vec = mm3(grown, protos[...], NT)
    lane = lax.broadcasted_iota(jnp.int32, (5, 128), 1)
    tops = jnp.where(lane == 0, top, jnp.where(lane == 1, size, 0.0))
    for peer in range(FRAMES):
        out[peer, 0:5, :] = vec[:, 0:128]
        out[peer, 5:10, :] = vec[:, 128:256]
        out[peer, 10:15, :] = tops
        out[peer, 15:19, :] = total[10:14]
        out[peer, 19:MSG, :] = jnp.zeros((MSG - 19, 128), F32)


def code_of(peak):
    return jnp.ceil(jnp.log(jnp.maximum(peak, 1e-30)) * (STEP / math.log(2.0))) + 1.0


def scale_of(code):
    return jnp.exp(code * (math.log(2.0) / STEP))


def whole_max(x):
    return jnp.max(jnp.max(x, axis=-1, keepdims=True), axis=0, keepdims=True)


def stack3(parts):
    return jnp.concatenate([piece for part in parts for piece in pieces(part)], axis=0)


def back_kernel(
    peers, got, zs, heads, ms, keep_own, keep_oth, query_own, query_oth, key_own, key_oth, taken_own, taken_oth,
    crow, flip_own, flip_oth, out, grad, rhs, last, line,
):
    tops = [got[source, 10:15, 0:1] for source in range(FRAMES)]
    top = functools.reduce(jnp.maximum, tops)
    size = jnp.zeros((5, 1), F32)
    low = jnp.zeros((5, 128), F32)
    high = jnp.zeros((5, 128), F32)
    for source in range(FRAMES):
        factor = jnp.exp(tops[source] - top)
        size = size + got[source, 10:15, 1:2] * factor
        low = low + got[source, 0:5, :] * factor
        high = high + got[source, 5:10, :] * factor
    expect = jnp.concatenate([low, high], axis=1) / size
    d_unit = (expect[0:4] - expect[4:5]) / (ALL_CLIPS * TAU_STUD)
    z_s = zs[...]
    inverse = rsqrt(jnp.sum(z_s * z_s, axis=-1, keepdims=True) + 1e-06)
    unit = z_s * inverse
    d_z = (d_unit - unit * jnp.sum(unit * d_unit, axis=-1, keepdims=True)) * inverse
    d_heads = mmh(d_z, ms[0], NT) / NTOK
    lane = lax.broadcasted_iota(jnp.int32, (ROWS, ROWS), 1)
    halves = ((keep_own, query_own, key_own, taken_own), (keep_oth, query_oth, key_oth, taken_oth))
    for half, (keep, by_query, by_key, received) in enumerate(halves):
        for tile in range(TILES):
            d_weights = mm3(d_heads, keep[2, tile], NT).astype(BF16).astype(F32)
            d_down = jnp.transpose(jnp.concatenate([d_weights, d_weights], axis=0))
            inner = jnp.zeros((ROWS, ROWS), F32)
            grow_q = []
            for clip in range(CLIPS):
                share = by_query[tile, clip]
                d_w = d_weights[clip : clip + 1, :]
                mean = jnp.sum(share * d_w, axis=-1, keepdims=True)
                inner = jnp.where(lane == clip, mean, inner)
                grow_q.append(share * (d_w - mean) * SCALE)
            inner = jnp.transpose(inner)
            grow_k = [
                by_key[tile, clip] * (d_down[:, clip : clip + 1] - inner[clip : clip + 1, :]) * SCALE
                for clip in range(CLIPS)
            ]
            wide_q = mm(stack3(grow_q), keep[1, tile])
            wide_k = mm(stack3(grow_k), keep[0, tile])
            totals = [jnp.zeros((ROWS, HS), F32) for _ in range(3)]
            for clip in range(CLIPS):
                many = crow[:, clip : clip + 1]
                first = 3 * clip * ROWS
                parts = [
                    wide[first : first + ROWS] + (wide[first + ROWS : first + 2 * ROWS] + wide[first + 2 * ROWS : first + 3 * ROWS])
                    for wide in (wide_q, wide_k)
                ]
                parts.append(received[tile, :, clip : clip + 1] * d_heads[clip : clip + 1, :])
                totals = [total + many * part.astype(BF16).astype(F32) for total, part in zip(totals, parts)]
            packed = jnp.concatenate(totals, axis=1)
            first = packed.astype(BF16)
            second = (packed - first.astype(F32)).astype(BF16)
            rows = pl.ds((half * TILES + tile) * ROWS, ROWS)
            rhs[rows, 0:256] = first[:, 0:256]
            rhs[rows, 256:512] = second[:, 0:256]
            rhs[rows, 512:528] = jnp.concatenate([first[:, 256:264], second[:, 256:264]], axis=1)
    count = TILES * ROWS
    wide = mm(flip_own[...], rhs[0:count, :]) + mm(flip_oth[...], rhs[count : 2 * count, :])
    main = wide[:, 0:256] + wide[:, 256:512]
    thin = jnp.transpose(wide[:, 512:520] + wide[:, 520:528])
    code = code_of(jnp.max(jnp.abs(main), axis=0, keepdims=True))
    grad[...] = jnp.round(main * (32000.0 / scale_of(code)))
    code_thin = code_of(jnp.max(jnp.abs(thin), axis=-1, keepdims=True))
    last[...] = jnp.round(thin * (32000.0 / scale_of(code_thin)))
    code_z = code_of(whole_max(jnp.abs(d_z)))
    sent_z = jnp.round(d_z * (32000.0 / scale_of(code_z)))
    mine = heads[...]
    code_h = code_of(whole_max(jnp.abs(mine)))
    sent_h = jnp.round(mine * (32000.0 / scale_of(code_h)))
    pooled = jnp.concatenate([got[source, 15:19, 0:HS] for source in range(FRAMES)], axis=1)
    code_p = code_of(whole_max(jnp.abs(pooled)))
    sent_p = jnp.round(pooled * (32000.0 / scale_of(code_p)))
    lane = lax.broadcasted_iota(jnp.int32, (1, 128), 1)
    codes = jnp.where(lane == 64, code_z, jnp.where(lane == 65, code_h, jnp.where(lane == 66, code_p, 0.0)))
    block = D // peers
    line[...] = jnp.zeros((QROWS, 256), F32)
    line[44:48, :] = sent_z
    line[48:49, 0:HS] = sent_h[0:1]
    line[48:49, 128 : 128 + HS] = sent_h[1:2]
    line[49:50, 0:HS] = sent_h[2:3]
    line[49:50, 128 : 128 + HS] = sent_h[3:4]
    line[55:56, :] = code
    for peer in range(peers):
        line[0:block, :] = grad[peer * block : (peer + 1) * block, :]
        part = sent_p[:, peer * block : (peer + 1) * block]
        line[50:54, 0:block] = part
        thin_part = last[:, peer * block : (peer + 1) * block]
        line[50:54, 64 : 64 + block] = thin_part[0:4]
        line[50:54, 128 : 128 + block] = thin_part[4:8]
        line[50:54, 192:193] = code_thin[0:4]
        line[50:54, 193:194] = code_thin[4:8]
        line[54:55, 0:128] = codes
        out[peer] = line[...].astype(jnp.int32).astype(jnp.int16)


def final_kernel(peers, got, bottle, g_qkv, g_out, g_bottle, z_all, h_all, p_all):
    block = D // peers
    main = jnp.zeros((block, 256), F32)
    thin_a = jnp.zeros((4, block), F32)
    thin_b = jnp.zeros((4, block), F32)
    for source in range(peers):
        line = got[source].astype(jnp.int32).astype(F32)
        main = main + line[0:block] * (scale_of(line[55:56]) / 32000.0)
        thin_a = thin_a + line[50:54, 64 : 64 + block] * (scale_of(line[50:54, 192:193]) / 32000.0)
        thin_b = thin_b + line[50:54, 128 : 128 + block] * (scale_of(line[50:54, 193:194]) / 32000.0)
        scales = scale_of(line[54:55, 0:128]) / 32000.0
        first = source * CLIPS
        z_all[first : first + 4, :] = line[44:48] * scales[:, 64:65]
        scale_h = scales[:, 65:66]
        h_all[first : first + 1, :] = line[48:49, 0:HS] * scale_h
        h_all[first + 1 : first + 2, :] = line[48:49, 128 : 128 + HS] * scale_h
        h_all[first + 2 : first + 3, :] = line[49:50, 0:HS] * scale_h
        h_all[first + 3 : first + 4, :] = line[49:50, 128 : 128 + HS] * scale_h
        p_all[first : first + 4, :] = line[50:54, 0:block] * scales[:, 66:67]
    g_qkv[:, 0:256] = main
    g_qkv[:, 256:264] = jnp.transpose(jnp.concatenate([thin_a, thin_b], axis=0))
    d_z = z_all[...]
    g_bottle[...] = mmh(p_all[...], d_z, TN)
    g_out[...] = mmh(bottle[...].astype(F32), mmh(h_all[...], d_z, TN), NT)


def local(
    global_clips,
    frame_map,
    teacher_qkv,
    teacher_out,
    teacher_bottle,
    student_qkv,
    student_out,
    student_bottle,
    prototypes,
    center,
):
    frame = lax.axis_index("frame")
    peers = lax.axis_size("crop") * lax.axis_size("dp")
    crops = lax.axis_size("crop")
    swap = [(index, index ^ 1) for index in range(FRAMES)]
    tokens = global_clips[0, 0]
    halves = jnp.broadcast_to(tokens.reshape(1, 2, 32, D), (FRAMES // 2, 2, 32, D)).reshape(FRAMES, 32, D)
    mixed = lax.all_to_all(halves, "frame", 0, 0, tiled=True)
    t_own = teacher_qkv.T
    s_own = student_qkv.T
    t_oth = lax.ppermute(t_own, "frame", swap)
    s_oth = lax.ppermute(s_own, "frame", swap)
    t_out_oth = lax.ppermute(teacher_out, "frame", swap)
    s_out_oth = lax.ppermute(student_out, "frame", swap)
    mt, ms, otz, zlocal, plocal, ccol, crow = call(
        prep_kernel,
        [
            ((2, HS, BOTTLE), F32),
            ((2, HS, BOTTLE), F32),
            ((1, BOTTLE), F32),
            ((CLIPS, BOTTLE), F32),
            ((CLIPS, D), F32),
            ((CLIPS, ROWS), F32),
            ((ROWS, ROWS), F32),
        ],
        frame_map[0], frame.astype(jnp.int32).reshape(1),
        tokens, teacher_out, t_out_oth, student_out, s_out_oth, teacher_bottle, student_bottle,
        smem=2,
    )
    normed, zt = call(
        teacher_kernel,
        [((TILES, ROWS, D), BF16), ((crops, 1, BOTTLE), F32)],
        mixed, t_own, t_oth, mt, otz,
    )
    ztc = lax.all_to_all(zt, "crop", 0, 0, tiled=True)
    keep_shape = (3, TILES, ROWS, HS)
    own, oth, zs, pooled, heads = call(
        student_kernel,
        [
            (keep_shape, BF16),
            (keep_shape, BF16),
            ((CLIPS, BOTTLE), F32),
            ((CLIPS, D), F32),
            ((2, CLIPS, HS), F32),
        ],
        normed, s_own, s_oth, ms, student_out, s_out_oth, zlocal, plocal, ccol, crow,
    )
    kept_oth = lax.ppermute(oth, "frame", swap)
    normed_oth = lax.ppermute(normed, "frame", swap)
    (sent,) = call(
        message_kernel,
        [((FRAMES, MSG, 128), F32)],
        frame.astype(jnp.int32).reshape(1), zs, ztc, pooled, heads, smem=1,
    )
    got = lax.all_to_all(sent, "frame", 0, 0, tiled=True)
    shares = [
        call(
            shares_kernel,
            [((TILES, CLIPS, ROWS, ROWS), F32), ((TILES, CLIPS, ROWS, ROWS), F32), ((TILES, ROWS, ROWS), F32)],
            keep, ccol, crow,
        )
        for keep in (own, kept_oth)
    ]
    flips = [call(flip_kernel, [((D, TILES * ROWS), BF16)], half)[0] for half in (normed, normed_oth)]
    sent, z_s, my_heads = call(
        logits_kernel,
        [((FRAMES, MSG, 128), F32), ((CLIPS, BOTTLE), F32), ((CLIPS, HS), F32)],
        got, prototypes, center.reshape(1, -1),
    )
    got = lax.all_to_all(sent, "frame", 0, 0, tiled=True)
    (sent,) = call(
        functools.partial(back_kernel, peers),
        [((peers, QROWS, 256), jnp.int16)],
        got, z_s, my_heads, ms, own, kept_oth,
        shares[0][0], shares[1][0], shares[0][1], shares[1][1], shares[0][2], shares[1][2],
        crow, flips[0], flips[1],
        scratch=[
            pltpu.VMEM((D, 256), F32),
            pltpu.VMEM((2 * TILES * ROWS, 528), BF16),
            pltpu.VMEM((8, D), F32),
            pltpu.VMEM((QROWS, 256), F32),
        ],
    )
    got = lax.all_to_all(sent, ("crop", "dp"), 0, 0, tiled=True)
    block = D // peers
    place = lax.axis_index("crop") * lax.axis_size("dp") + lax.axis_index("dp")
    bottle = lax.dynamic_slice_in_dim(student_bottle, place * block, block, axis=0)
    g_qkv, g_out, g_bottle = call(
        functools.partial(final_kernel, peers),
        [((block, 3 * HS), F32), ((block, HS), F32), ((block, BOTTLE), F32)],
        got, bottle,
        scratch=[
            pltpu.VMEM((peers * CLIPS, BOTTLE), F32),
            pltpu.VMEM((peers * CLIPS, HS), F32),
            pltpu.VMEM((peers * CLIPS, block), F32),
        ],
    )
    return g_qkv, g_out.T, g_bottle


def solution(mesh):
    return jax.shard_map(
        local,
        mesh=mesh,
        in_specs=(
            P("dp", "frame", "crop", None),
            P("dp", "crop", None),
            P(None, "frame"),
            P("frame", None),
            P(),
            P(None, "frame"),
            P("frame", None),
            P(),
            P(None, "frame"),
            P("frame"),
        ),
        out_specs=(P(("crop", "dp"), "frame"), P("frame", ("crop", "dp")), P(("crop", "dp"), None)),
        check_vma=False,
    )
```

```python
import functools
import math

import jax
import jax.numpy as jnp
from jax import lax
from jax.experimental import pallas as pl
from jax.experimental.pallas import tpu as pltpu
from jax.sharding import PartitionSpec as P

D = 1408
HEADS = 16
HS = 88
FRAMES = 16
BOTTLE = 256
GP = 8
ROWS = FRAMES * GP
TILES = 4
LFRAMES = 8
CLIPS = 4
NTOK = 512
NTEACH = 4096
TAU_TEACH = 0.04
TAU_STUD = 0.1
ALL_CLIPS = 16
HIGH = lax.Precision.HIGHEST
F32 = jnp.float32
BF16 = jnp.bfloat16
NEG = -1e30
SCALE = 1.0 / math.sqrt(HS)
MSG = 24
QROWS = 56
STEP = 64.0
INTERPRET = False

NN = (((1,), (0,)), ((), ()))
NT = (((1,), (1,)), ((), ()))
TN = (((0,), (0,)), ((), ()))


def call(kernel, outs, *args, scratch=(), smem=0, hbm_in=(), hbm_out=(), limit=16):
    def space(index, in_hbm):
        return pl.BlockSpec(memory_space=pltpu.HBM if index in in_hbm else pltpu.VMEM)

    spec = [pl.BlockSpec(memory_space=pltpu.SMEM)] * smem
    spec += [space(index, hbm_in) for index in range(smem, len(args))]
    args = [pltpu.with_memory_space_constraint(arg, pltpu.HBM) if index in hbm_in else arg for index, arg in enumerate(args)]
    return pl.pallas_call(
        kernel,
        out_shape=tuple(
            pltpu.HBM(shape, dtype) if index in hbm_out else jax.ShapeDtypeStruct(shape, dtype)
            for index, (shape, dtype) in enumerate(outs)
        ),
        in_specs=spec,
        out_specs=tuple(space(index, hbm_out) for index in range(len(outs))),
        scratch_shapes=list(scratch),
        compiler_params=pltpu.CompilerParams(vmem_limit_bytes=limit * 2**20),
        interpret=INTERPRET,
    )(*args)


def room(*arrays):
    held = [pltpu.VMEM(tuple(array.shape), array.dtype) for array in arrays]
    return held + [pltpu.SemaphoreType.DMA((len(held),))]


def begin(sources, targets, sems):
    copies = [pltpu.make_async_copy(source, target, sems.at[i]) for i, (source, target) in enumerate(zip(sources, targets))]
    for copy in copies:
        copy.start()
    return copies


def mm(a, b, dims=NN):
    return lax.dot_general(a, b, dims, preferred_element_type=F32)


def mmh(a, b, dims=NN):
    return lax.dot_general(a, b, dims, precision=HIGH, preferred_element_type=F32)


def pieces(x):
    top = x.astype(BF16)
    rest = x - top.astype(F32)
    mid = rest.astype(BF16)
    return top, mid, (rest - mid.astype(F32)).astype(BF16)


def mm3(x, y, dims=NN):
    top, mid, low = pieces(x)
    return mm(top, y, dims) + (mm(mid, y, dims) + mm(low, y, dims))


def rsqrt(x):
    guess = lax.rsqrt(x)
    return guess * (1.5 - 0.5 * x * guess * guess)


def same_patch():
    row = lax.broadcasted_iota(jnp.int32, (ROWS, ROWS), 0)
    col = lax.broadcasted_iota(jnp.int32, (ROWS, ROWS), 1)
    return jnp.where((row % GP) == (col % GP), 0.0, NEG).astype(F32)


def split_qkv(flat):
    rounded = flat.astype(BF16)
    return rounded[:, :HS], rounded[:, HS : 2 * HS], rounded[:, 2 * HS :]


def spread_kernel(tok, out, sems):
    half = out.shape[1]
    copies = [
        pltpu.make_async_copy(tok.at[pl.ds((peer % 2) * half, half)], out.at[peer], sems.at[peer])
        for peer in range(FRAMES)
    ]
    for copy in copies:
        copy.start()
    for copy in copies:
        copy.wait()


def prep_kernel(
    maps, frame, tok, t_out, t_oth, s_out, s_oth, t_bot, s_bot, mt, ms, otz, zlocal, plocal, ccol, crow
):
    total = jnp.sum(tok[...].astype(F32), axis=0, keepdims=True)
    otz[...] = mm3(total, t_bot[...])
    osz = mm3(total, s_bot[...])
    mt[0] = mm(t_out[...], t_bot[...])
    mt[1] = mm(t_oth[...], t_bot[...])
    ms[0] = mm(s_out[...], s_bot[...])
    ms[1] = mm(s_oth[...], s_bot[...])
    lane = lax.broadcasted_iota(jnp.int32, (1, ROWS), 1)
    row = lax.broadcasted_iota(jnp.int32, (ROWS, ROWS), 0) // GP
    down = jnp.zeros((ROWS, ROWS), F32)
    across = [jnp.zeros((1, ROWS), F32) for _ in range(CLIPS)]
    mine = [jnp.zeros((1, ROWS), F32) for _ in range(CLIPS)]
    for step in range(LFRAMES):
        shown = jnp.full((1, ROWS), -1, jnp.int32)
        for clip in range(CLIPS):
            index = maps[clip, step]
            shown = jnp.where(lane == clip, index, shown)
            across[clip] = across[clip] + jnp.where(lane // GP == index, 1.0, 0.0)
            mine[clip] = mine[clip] + jnp.where(index == frame[0], 1.0, 0.0)
        down = down + jnp.where(row == shown, 1.0, 0.0)
    crow[...] = down
    for clip in range(CLIPS):
        ccol[clip : clip + 1, :] = across[clip]
        frac = mine[clip][:, 0:1] / NTOK
        zlocal[clip : clip + 1, :] = frac * osz
        plocal[clip : clip + 1, :] = frac * total


def teacher_kernel(x, w_own_far, w_oth_far, mt_far, otz, normed, zt, w_own, w_oth, mt, sems):
    copies = begin((w_own_far, w_oth_far, mt_far), (w_own, w_oth, mt), sems)
    for group in range(2):
        values = x[:, group * 2 * GP : (group + 1) * 2 * GP, :].astype(F32)
        middle = jnp.mean(values, axis=-1, keepdims=True)
        moved = values - middle
        spread = jnp.mean(moved * moved, axis=-1, keepdims=True)
        token = moved * rsqrt(spread + 1e-06)
        normed[2 * group] = token[:, :GP].reshape(ROWS, D).astype(BF16)
        normed[2 * group + 1] = token[:, GP:].reshape(ROWS, D).astype(BF16)
    mask = same_patch()
    tokens = normed[...].reshape(TILES * ROWS, D)
    total = otz[...]
    copies[2].wait()
    for head, weight in enumerate((w_own, w_oth)):
        copies[head].wait()
        flat = mm(tokens, weight[...], NT)
        summed = jnp.zeros((1, HS), F32)
        for tile in range(TILES):
            query, key, value = split_qkv(flat[tile * ROWS : (tile + 1) * ROWS])
            scores = mm(query, key, NT) * SCALE + mask
            scores = jnp.exp(scores - jnp.max(scores, axis=-1, keepdims=True))
            share = scores / jnp.sum(scores, axis=-1, keepdims=True)
            att = mm(share.astype(BF16), value)
            summed = summed + jnp.sum(att, axis=0, keepdims=True)
        total = total + mmh(summed, mt[head])
    for crop in range(zt.shape[0]):
        zt[crop] = total / NTEACH


def clip_shares(scores, count):
    here = jnp.where(count > 0.0, scores, NEG)
    here = jnp.exp(here - jnp.max(here, axis=-1, keepdims=True))
    return here / jnp.sum(here * count, axis=-1, keepdims=True)


def student_kernel(
    normed, w_own_far, w_oth_far, ms_far, s_out_far, s_oth_far, zlocal, plocal, ccol, crow,
    own_far, oth_far, shares_own_far, shares_oth_far, zs, pooled, heads,
    w_own, w_oth, ms, s_out, s_oth, sems, own, oth, shares_own, shares_oth, out_sems,
):
    copies = begin((w_own_far, w_oth_far, ms_far, s_out_far, s_oth_far), (w_own, w_oth, ms, s_out, s_oth), sems)
    mask = same_patch()
    tokens = normed[...].reshape(TILES * ROWS, D)
    leaving = []
    sides = ((w_own, own, shares_own, own_far, shares_own_far), (w_oth, oth, shares_oth, oth_far, shares_oth_far))
    for head, (weight, keep, shares, keep_far, shares_far) in enumerate(sides):
        copies[head].wait()
        flat = mm(tokens, weight[...], NT)
        summed = jnp.zeros((CLIPS, HS), F32)
        for tile in range(TILES):
            query, key, value = split_qkv(flat[tile * ROWS : (tile + 1) * ROWS])
            keep[0, tile] = query
            keep[1, tile] = key
            keep[2, tile] = value
            scores = mm(query, key, NT) * SCALE + mask
            totals = []
            for clip in range(CLIPS):
                count = ccol[clip : clip + 1, :]
                share = clip_shares(scores, count)
                shares[tile, clip] = share
                share = share.astype(BF16).astype(F32) * crow[:, clip : clip + 1]
                totals.append(jnp.sum(share, axis=0, keepdims=True) * count)
            summed = summed + mm3(jnp.concatenate(totals, axis=0), value)
        leaving += begin((keep, shares), (keep_far, shares_far), out_sems.at[pl.ds(2 * head, 2)])
        heads[head] = summed / NTOK
    for copy in copies[2:]:
        copy.wait()
    zs[...] = mmh(heads[0], ms[0]) + mmh(heads[1], ms[1]) + zlocal[...]
    pooled[...] = mm3(heads[0], s_out[...]) + mm3(heads[1], s_oth[...]) + plocal[...]
    for copy in leaving:
        copy.wait()


def flip_kernel(normed_far, normed_oth_far, out_own_far, out_oth_far, half, half_oth, sems, out_own, out_oth, out_sems):
    copies = begin((normed_far, normed_oth_far), (half, half_oth), sems)
    leaving = []
    for index, (held, out, far) in enumerate(((half, out_own, out_own_far), (half_oth, out_oth, out_oth_far))):
        copies[index].wait()
        out[...] = jnp.transpose(held[...].reshape(TILES * ROWS, D))
        leaving += begin((out,), (far,), out_sems.at[pl.ds(index, 1)])
    for copy in leaving:
        copy.wait()


def message_kernel(frame, zs, ztc, pooled, heads, out):
    me = frame[0]
    zt = jnp.sum(ztc[...], axis=0)
    for peer in range(FRAMES):
        out[peer, 0:4, :] = zs[:, 0:128]
        out[peer, 4:8, :] = zs[:, 128:256]
        out[peer, 8:9, :] = zt[:, 0:128]
        out[peer, 9:10, :] = zt[:, 128:256]
        out[peer, 10:MSG, :] = jnp.zeros((MSG - 10, 128), F32)
        out[peer, 10:14, 0:HS] = pooled[:, peer * HS : (peer + 1) * HS]
        mine = (me == peer).astype(F32)
        partner = (jnp.bitwise_xor(me, 1) == peer).astype(F32)
        out[peer, 14:18, 0:HS] = heads[0] * mine + heads[1] * partner


def logits_kernel(got, protos, center, out, zs, heads):
    total = got[0]
    for source in range(1, FRAMES):
        total = total + got[source]
    z_s = jnp.concatenate([total[0:4], total[4:8]], axis=1)
    z_t = jnp.concatenate([total[8:9], total[9:10]], axis=1)
    zs[...] = z_s
    heads[...] = total[14:18, 0:HS]
    z_all = jnp.concatenate([z_s, z_t], axis=0)
    unit = z_all * rsqrt(jnp.sum(z_all * z_all, axis=-1, keepdims=True) + 1e-06)
    wide = mm3(unit, protos[...])
    logits = jnp.concatenate([wide[0:4] / TAU_STUD, (wide[4:5] - center[...]) / TAU_TEACH], axis=0)
    top = jnp.max(logits, axis=-1, keepdims=True)
    grown = jnp.exp(logits - top)
    size = jnp.sum(grown, axis=-1, keepdims=True)
    vec = mm3(grown, protos[...], NT)
    lane = lax.broadcasted_iota(jnp.int32, (5, 128), 1)
    tops = jnp.where(lane == 0, top, jnp.where(lane == 1, size, 0.0))
    for peer in range(FRAMES):
        out[peer, 0:5, :] = vec[:, 0:128]
        out[peer, 5:10, :] = vec[:, 128:256]
        out[peer, 10:15, :] = tops
        out[peer, 15:19, :] = total[10:14]
        out[peer, 19:MSG, :] = jnp.zeros((MSG - 19, 128), F32)


def code_of(peak):
    return jnp.ceil(jnp.log(jnp.maximum(peak, 1e-30)) * (STEP / math.log(2.0))) + 1.0


def scale_of(code):
    return jnp.exp(code * (math.log(2.0) / STEP))


def whole_max(x):
    return jnp.max(jnp.max(x, axis=-1, keepdims=True), axis=0, keepdims=True)


def stack3(parts):
    return jnp.concatenate([piece for part in parts for piece in pieces(part)], axis=0)


def back_kernel(
    peers, got, zs, heads, ms, own_far, oth_far, shares_own_far, shares_oth_far,
    ccol, crow, flip_own_far, flip_oth_far, out_far,
    keep_own, shares_own, keep_oth, shares_oth, flip_own, flip_oth, sems, out, out_sems, grad, rhs, last, line,
):
    copies = begin(
        (own_far, shares_own_far, oth_far, shares_oth_far, flip_own_far, flip_oth_far),
        (keep_own, shares_own, keep_oth, shares_oth, flip_own, flip_oth),
        sems,
    )
    tops = [got[source, 10:15, 0:1] for source in range(FRAMES)]
    top = functools.reduce(jnp.maximum, tops)
    size = jnp.zeros((5, 1), F32)
    low = jnp.zeros((5, 128), F32)
    high = jnp.zeros((5, 128), F32)
    for source in range(FRAMES):
        factor = jnp.exp(tops[source] - top)
        size = size + got[source, 10:15, 1:2] * factor
        low = low + got[source, 0:5, :] * factor
        high = high + got[source, 5:10, :] * factor
    expect = jnp.concatenate([low, high], axis=1) / size
    d_unit = (expect[0:4] - expect[4:5]) / (ALL_CLIPS * TAU_STUD)
    z_s = zs[...]
    inverse = rsqrt(jnp.sum(z_s * z_s, axis=-1, keepdims=True) + 1e-06)
    unit = z_s * inverse
    d_z = (d_unit - unit * jnp.sum(unit * d_unit, axis=-1, keepdims=True)) * inverse
    d_heads = mmh(d_z, ms[0], NT) / NTOK
    lane = lax.broadcasted_iota(jnp.int32, (ROWS, ROWS), 1)
    for half, (keep, shares) in enumerate(((keep_own, shares_own), (keep_oth, shares_oth))):
        copies[2 * half].wait()
        copies[2 * half + 1].wait()
        for tile in range(TILES):
            d_weights = mm3(d_heads, keep[2, tile], NT).astype(BF16).astype(F32)
            taken = [
                jnp.sum(shares[tile, clip].astype(BF16).astype(F32) * crow[:, clip : clip + 1], axis=0, keepdims=True)
                for clip in range(CLIPS)
            ]
            d_down = jnp.transpose(jnp.concatenate([d_weights] + taken, axis=0))
            inner = jnp.zeros((ROWS, ROWS), F32)
            grow_q = []
            for clip in range(CLIPS):
                share = shares[tile, clip] * ccol[clip : clip + 1, :]
                d_w = d_weights[clip : clip + 1, :]
                mean = jnp.sum(share * d_w, axis=-1, keepdims=True)
                inner = jnp.where(lane == clip, mean, inner)
                grow_q.append(share * (d_w - mean) * SCALE)
            inner = jnp.transpose(inner)
            grow_k = [
                jnp.transpose(shares[tile, clip])
                * ccol[clip : clip + 1, :]
                * (d_down[:, clip : clip + 1] - inner[clip : clip + 1, :])
                * SCALE
                for clip in range(CLIPS)
            ]
            wide_q = mm(stack3(grow_q), keep[1, tile])
            wide_k = mm(stack3(grow_k), keep[0, tile])
            totals = [jnp.zeros((ROWS, HS), F32) for _ in range(3)]
            for clip in range(CLIPS):
                many = crow[:, clip : clip + 1]
                first = 3 * clip * ROWS
                parts = [
                    wide[first : first + ROWS] + (wide[first + ROWS : first + 2 * ROWS] + wide[first + 2 * ROWS : first + 3 * ROWS])
                    for wide in (wide_q, wide_k)
                ]
                parts.append(d_down[:, CLIPS + clip : CLIPS + clip + 1] * d_heads[clip : clip + 1, :])
                totals = [total + many * part.astype(BF16).astype(F32) for total, part in zip(totals, parts)]
            packed = jnp.concatenate(totals, axis=1)
            first = packed.astype(BF16)
            second = (packed - first.astype(F32)).astype(BF16)
            rows = pl.ds((half * TILES + tile) * ROWS, ROWS)
            rhs[rows, 0:256] = first[:, 0:256]
            rhs[rows, 256:512] = second[:, 0:256]
            rhs[rows, 512:528] = jnp.concatenate([first[:, 256:264], second[:, 256:264]], axis=1)
    count = TILES * ROWS
    copies[4].wait()
    copies[5].wait()
    wide = mm(flip_own[...], rhs[0:count, :]) + mm(flip_oth[...], rhs[count : 2 * count, :])
    main = wide[:, 0:256] + wide[:, 256:512]
    thin = jnp.transpose(wide[:, 512:520] + wide[:, 520:528])
    code = code_of(jnp.max(jnp.abs(main), axis=0, keepdims=True))
    grad[...] = jnp.round(main * (32000.0 / scale_of(code)))
    code_thin = code_of(jnp.max(jnp.abs(thin), axis=-1, keepdims=True))
    last[...] = jnp.round(thin * (32000.0 / scale_of(code_thin)))
    code_z = code_of(whole_max(jnp.abs(d_z)))
    sent_z = jnp.round(d_z * (32000.0 / scale_of(code_z)))
    mine = heads[...]
    code_h = code_of(whole_max(jnp.abs(mine)))
    sent_h = jnp.round(mine * (32000.0 / scale_of(code_h)))
    pooled = jnp.concatenate([got[source, 15:19, 0:HS] for source in range(FRAMES)], axis=1)
    code_p = code_of(whole_max(jnp.abs(pooled)))
    sent_p = jnp.round(pooled * (32000.0 / scale_of(code_p)))
    lane = lax.broadcasted_iota(jnp.int32, (1, 128), 1)
    codes = jnp.where(lane == 64, code_z, jnp.where(lane == 65, code_h, jnp.where(lane == 66, code_p, 0.0)))
    block = D // peers
    line[...] = jnp.zeros((QROWS, 256), F32)
    line[44:48, :] = sent_z
    line[48:49, 0:HS] = sent_h[0:1]
    line[48:49, 128 : 128 + HS] = sent_h[1:2]
    line[49:50, 0:HS] = sent_h[2:3]
    line[49:50, 128 : 128 + HS] = sent_h[3:4]
    line[55:56, :] = code
    leaving = []
    for peer in range(peers):
        line[0:block, :] = grad[peer * block : (peer + 1) * block, :]
        part = sent_p[:, peer * block : (peer + 1) * block]
        line[50:54, 0:block] = part
        thin_part = last[:, peer * block : (peer + 1) * block]
        line[50:54, 64 : 64 + block] = thin_part[0:4]
        line[50:54, 128 : 128 + block] = thin_part[4:8]
        line[50:54, 192:193] = code_thin[0:4]
        line[50:54, 193:194] = code_thin[4:8]
        line[54:55, 0:128] = codes
        out[peer] = line[...].astype(jnp.int32).astype(jnp.int16)
        leaving += begin((out.at[peer],), (out_far.at[peer],), out_sems.at[pl.ds(peer, 1)])
    for copy in leaving:
        copy.wait()


def final_kernel(peers, got, bottle, g_qkv, g_out, g_bottle, z_all, h_all, p_all):
    block = D // peers
    main = jnp.zeros((block, 256), F32)
    thin_a = jnp.zeros((4, block), F32)
    thin_b = jnp.zeros((4, block), F32)
    for source in range(peers):
        line = got[source].astype(jnp.int32).astype(F32)
        main = main + line[0:block] * (scale_of(line[55:56]) / 32000.0)
        thin_a = thin_a + line[50:54, 64 : 64 + block] * (scale_of(line[50:54, 192:193]) / 32000.0)
        thin_b = thin_b + line[50:54, 128 : 128 + block] * (scale_of(line[50:54, 193:194]) / 32000.0)
        scales = scale_of(line[54:55, 0:128]) / 32000.0
        first = source * CLIPS
        z_all[first : first + 4, :] = line[44:48] * scales[:, 64:65]
        scale_h = scales[:, 65:66]
        h_all[first : first + 1, :] = line[48:49, 0:HS] * scale_h
        h_all[first + 1 : first + 2, :] = line[48:49, 128 : 128 + HS] * scale_h
        h_all[first + 2 : first + 3, :] = line[49:50, 0:HS] * scale_h
        h_all[first + 3 : first + 4, :] = line[49:50, 128 : 128 + HS] * scale_h
        p_all[first : first + 4, :] = line[50:54, 0:block] * scales[:, 66:67]
    g_qkv[:, 0:256] = main
    g_qkv[:, 256:264] = jnp.transpose(jnp.concatenate([thin_a, thin_b], axis=0))
    d_z = z_all[...]
    g_bottle[...] = mmh(p_all[...], d_z, TN)
    g_out[...] = mmh(bottle[...].astype(F32), mmh(h_all[...], d_z, TN), NT)


def local(
    global_clips,
    frame_map,
    teacher_qkv,
    teacher_out,
    teacher_bottle,
    student_qkv,
    student_out,
    student_bottle,
    prototypes,
    center,
):
    frame = lax.axis_index("frame")
    peers = lax.axis_size("crop") * lax.axis_size("dp")
    crops = lax.axis_size("crop")
    swap = [(index, index ^ 1) for index in range(FRAMES)]
    tokens = global_clips[0, 0]
    (spread,) = call(
        spread_kernel,
        [((FRAMES, tokens.shape[0] // 2, D), BF16)],
        tokens,
        hbm_in=(0,), hbm_out=(0,), scratch=[pltpu.SemaphoreType.DMA((FRAMES,))],
    )
    mixed = lax.all_to_all(spread, "frame", 0, 0, tiled=True)
    t_own = teacher_qkv.T
    s_own = student_qkv.T
    t_oth = lax.ppermute(t_own, "frame", swap)
    s_oth = lax.ppermute(s_own, "frame", swap)
    t_out_oth = lax.ppermute(teacher_out, "frame", swap)
    s_out_oth = lax.ppermute(student_out, "frame", swap)
    mt, ms, otz, zlocal, plocal, ccol, crow = call(
        prep_kernel,
        [
            ((2, HS, BOTTLE), F32),
            ((2, HS, BOTTLE), F32),
            ((1, BOTTLE), F32),
            ((CLIPS, BOTTLE), F32),
            ((CLIPS, D), F32),
            ((CLIPS, ROWS), F32),
            ((ROWS, ROWS), F32),
        ],
        frame_map[0], frame.astype(jnp.int32).reshape(1),
        tokens, teacher_out, t_out_oth, student_out, s_out_oth, teacher_bottle, student_bottle,
        smem=2,
    )
    normed, zt = call(
        teacher_kernel,
        [((TILES, ROWS, D), BF16), ((crops, 1, BOTTLE), F32)],
        mixed, t_own, t_oth, mt, otz,
        hbm_in=(1, 2, 3), scratch=room(t_own, t_oth, mt),
    )
    ztc = lax.all_to_all(zt, "crop", 0, 0, tiled=True)
    keep = jax.ShapeDtypeStruct((3, TILES, ROWS, HS), BF16)
    table = jax.ShapeDtypeStruct((TILES, CLIPS, ROWS, ROWS), F32)
    own, oth, shares_own, shares_oth, zs, pooled, heads = call(
        student_kernel,
        [
            (keep.shape, BF16),
            (keep.shape, BF16),
            (table.shape, F32),
            (table.shape, F32),
            ((CLIPS, BOTTLE), F32),
            ((CLIPS, D), F32),
            ((2, CLIPS, HS), F32),
        ],
        normed, s_own, s_oth, ms, student_out, s_out_oth, zlocal, plocal, ccol, crow,
        hbm_in=(1, 2, 3, 4, 5), hbm_out=(0, 1, 2, 3), limit=20,
        scratch=room(s_own, s_oth, ms, student_out, s_out_oth) + room(keep, keep, table, table),
    )
    (sent,) = call(
        message_kernel,
        [((FRAMES, MSG, 128), F32)],
        frame.astype(jnp.int32).reshape(1), zs, ztc, pooled, heads, smem=1,
    )
    sent, leaving = lax.optimization_barrier((sent, (normed, oth, shares_oth)))
    got = lax.all_to_all(sent, "frame", 0, 0, tiled=True)
    normed_oth, kept_oth, shares_got = (lax.ppermute(part, "frame", swap) for part in leaving)
    flat = jax.ShapeDtypeStruct((D, TILES * ROWS), BF16)
    flips = call(
        flip_kernel,
        [(flat.shape, BF16), (flat.shape, BF16)],
        normed, normed_oth,
        hbm_in=(0, 1), hbm_out=(0, 1), scratch=room(normed, normed_oth) + room(flat, flat),
    )
    sent, z_s, my_heads = call(
        logits_kernel,
        [((FRAMES, MSG, 128), F32), ((CLIPS, BOTTLE), F32), ((CLIPS, HS), F32)],
        got, prototypes, center.reshape(1, -1),
    )
    got = lax.all_to_all(sent, "frame", 0, 0, tiled=True)
    (sent,) = call(
        functools.partial(back_kernel, peers),
        [((peers, QROWS, 256), jnp.int16)],
        got, z_s, my_heads, ms, own, kept_oth, shares_own, shares_got, ccol, crow, flips[0], flips[1],
        hbm_in=(4, 5, 6, 7, 10, 11), hbm_out=(0,), limit=30,
        scratch=room(own, shares_own, kept_oth, shares_got, flips[0], flips[1])
        + [
            pltpu.VMEM((peers, QROWS, 256), jnp.int16),
            pltpu.SemaphoreType.DMA((peers,)),
            pltpu.VMEM((D, 256), F32),
            pltpu.VMEM((2 * TILES * ROWS, 528), BF16),
            pltpu.VMEM((8, D), F32),
            pltpu.VMEM((QROWS, 256), F32),
        ],
    )
    got = lax.all_to_all(sent, ("crop", "dp"), 0, 0, tiled=True)
    block = D // peers
    place = lax.axis_index("crop") * lax.axis_size("dp") + lax.axis_index("dp")
    bottle = lax.dynamic_slice_in_dim(student_bottle, place * block, block, axis=0)
    g_qkv, g_out, g_bottle = call(
        functools.partial(final_kernel, peers),
        [((block, 3 * HS), F32), ((block, HS), F32), ((block, BOTTLE), F32)],
        got, bottle,
        scratch=[
            pltpu.VMEM((peers * CLIPS, BOTTLE), F32),
            pltpu.VMEM((peers * CLIPS, HS), F32),
            pltpu.VMEM((peers * CLIPS, block), F32),
        ],
    )
    return g_qkv, g_out.T, g_bottle


def solution(mesh):
    return jax.shard_map(
        local,
        mesh=mesh,
        in_specs=(
            P("dp", "frame", "crop", None),
            P("dp", "crop", None),
            P(None, "frame"),
            P("frame", None),
            P(),
            P(None, "frame"),
            P("frame", None),
            P(),
            P(None, "frame"),
            P("frame"),
        ),
        out_specs=(P(("crop", "dp"), "frame"), P("frame", ("crop", "dp")), P(("crop", "dp"), None)),
        check_vma=False,
    )
```

```python
import functools
import math

import jax
import jax.numpy as jnp
from jax import lax
from jax.experimental import pallas as pl
from jax.experimental.pallas import tpu as pltpu
from jax.sharding import PartitionSpec as P


D = 1408
HS = 88
FRAMES = 16
BOTTLE = 256
GP = 8
ROWS = FRAMES * GP
TILES = 4
LFRAMES = 8
CLIPS = 4
NTOK = 512
NTEACH = 4096
TAU_TEACH = 0.04
TAU_STUD = 0.1
ALL_CLIPS = 16
HIGH = lax.Precision.HIGHEST
F32 = jnp.float32
BF16 = jnp.bfloat16
NEG = -1e30
SCALE = 1.0 / math.sqrt(HS)
MSG = 24
QROWS = 56
STEP = 64.0
INTERPRET = False

NN = (((1,), (0,)), ((), ()))
NT = (((1,), (1,)), ((), ()))
TN = (((0,), (0,)), ((), ()))


def call(kernel, outs, *args, scratch=(), smem=0, hbm_in=(), hbm_out=(), limit=16):
    def space(index, in_hbm):
        return pl.BlockSpec(memory_space=pltpu.HBM if index in in_hbm else pltpu.VMEM)

    spec = [pl.BlockSpec(memory_space=pltpu.SMEM)] * smem
    spec += [space(index, hbm_in) for index in range(smem, len(args))]
    args = [pltpu.with_memory_space_constraint(arg, pltpu.HBM) if index in hbm_in else arg for index, arg in enumerate(args)]
    return pl.pallas_call(
        kernel,
        out_shape=tuple(
            pltpu.HBM(shape, dtype) if index in hbm_out else jax.ShapeDtypeStruct(shape, dtype)
            for index, (shape, dtype) in enumerate(outs)
        ),
        in_specs=spec,
        out_specs=tuple(space(index, hbm_out) for index in range(len(outs))),
        scratch_shapes=list(scratch),
        compiler_params=pltpu.CompilerParams(vmem_limit_bytes=limit * 2**20),
        interpret=INTERPRET,
    )(*args)


def room(*arrays):
    held = [pltpu.VMEM(tuple(array.shape), array.dtype) for array in arrays]
    return held + [pltpu.SemaphoreType.DMA((len(held),))]


def begin(sources, targets, sems):
    copies = [pltpu.make_async_copy(source, target, sems.at[i]) for i, (source, target) in enumerate(zip(sources, targets))]
    for copy in copies:
        copy.start()
    return copies


def mm(a, b, dims=NN):
    return lax.dot_general(a, b, dims, preferred_element_type=F32)


def mmh(a, b, dims=NN):
    return lax.dot_general(a, b, dims, precision=HIGH, preferred_element_type=F32)


def pieces(x):
    top = x.astype(BF16)
    rest = x - top.astype(F32)
    mid = rest.astype(BF16)
    return top, mid, (rest - mid.astype(F32)).astype(BF16)


def mm3(x, y, dims=NN):
    top, mid, low = pieces(x)
    return mm(top, y, dims) + (mm(mid, y, dims) + mm(low, y, dims))


def rsqrt(x):
    guess = lax.rsqrt(x)
    return guess * (1.5 - 0.5 * x * guess * guess)


def same_patch():
    row = lax.broadcasted_iota(jnp.int32, (ROWS, ROWS), 0)
    col = lax.broadcasted_iota(jnp.int32, (ROWS, ROWS), 1)
    return jnp.where((row % GP) == (col % GP), 0.0, NEG).astype(F32)


def split_qkv(flat):
    rounded = flat.astype(BF16)
    return rounded[:, :HS], rounded[:, HS : 2 * HS], rounded[:, 2 * HS :]


def spread_kernel(tok, out):
    half = out.shape[1]
    for peer in range(FRAMES):
        out[peer] = tok[(peer % 2) * half : (peer % 2 + 1) * half, :]


def prep_kernel(
    maps, frame, tok, t_out, t_oth, s_out, s_oth, t_bot, s_bot, mt, ms, otz, zlocal, plocal, ccol, crow
):
    total = jnp.sum(tok[...].astype(F32), axis=0, keepdims=True)
    otz[...] = mm3(total, t_bot[...])
    osz = mm3(total, s_bot[...])
    mt[0] = mm(t_out[...], t_bot[...])
    mt[1] = mm(t_oth[...], t_bot[...])
    ms[0] = mm(s_out[...], s_bot[...])
    ms[1] = mm(s_oth[...], s_bot[...])
    lane = lax.broadcasted_iota(jnp.int32, (1, ROWS), 1)
    row = lax.broadcasted_iota(jnp.int32, (ROWS, ROWS), 0) // GP
    down = jnp.zeros((ROWS, ROWS), F32)
    across = [jnp.zeros((1, ROWS), F32) for _ in range(CLIPS)]
    mine = [jnp.zeros((1, ROWS), F32) for _ in range(CLIPS)]
    for step in range(LFRAMES):
        shown = jnp.full((1, ROWS), -1, jnp.int32)
        for clip in range(CLIPS):
            index = maps[clip, step]
            shown = jnp.where(lane == clip, index, shown)
            across[clip] = across[clip] + jnp.where(lane // GP == index, 1.0, 0.0)
            mine[clip] = mine[clip] + jnp.where(index == frame[0], 1.0, 0.0)
        down = down + jnp.where(row == shown, 1.0, 0.0)
    crow[...] = down
    for clip in range(CLIPS):
        ccol[clip : clip + 1, :] = across[clip]
        frac = mine[clip][:, 0:1] / NTOK
        zlocal[clip : clip + 1, :] = frac * osz
        plocal[clip : clip + 1, :] = frac * total


def teacher_kernel(x, w_own_far, w_oth_far, mt_far, otz, normed, zt, w_own, w_oth, mt, sems):
    copies = begin((w_own_far, w_oth_far, mt_far), (w_own, w_oth, mt), sems)
    for group in range(2):
        values = x[:, group * 2 * GP : (group + 1) * 2 * GP, :].astype(F32)
        middle = jnp.mean(values, axis=-1, keepdims=True)
        moved = values - middle
        spread = jnp.mean(moved * moved, axis=-1, keepdims=True)
        token = moved * rsqrt(spread + 1e-06)
        normed[2 * group] = token[:, :GP].reshape(ROWS, D).astype(BF16)
        normed[2 * group + 1] = token[:, GP:].reshape(ROWS, D).astype(BF16)
    mask = same_patch()
    tokens = normed[...].reshape(TILES * ROWS, D)
    total = otz[...]
    copies[2].wait()
    for head, weight in enumerate((w_own, w_oth)):
        copies[head].wait()
        flat = mm(tokens, weight[...], NT)
        summed = jnp.zeros((1, HS), F32)
        for tile in range(TILES):
            query, key, value = split_qkv(flat[tile * ROWS : (tile + 1) * ROWS])
            scores = mm(query, key, NT) * SCALE + mask
            scores = jnp.exp(scores - jnp.max(scores, axis=-1, keepdims=True))
            share = scores / jnp.sum(scores, axis=-1, keepdims=True)
            att = mm(share.astype(BF16), value)
            summed = summed + jnp.sum(att, axis=0, keepdims=True)
        total = total + mmh(summed, mt[head])
    for crop in range(zt.shape[0]):
        zt[crop] = total / NTEACH


def clip_shares(scores, count):
    here = jnp.where(count > 0.0, scores, NEG)
    here = jnp.exp(here - jnp.max(here, axis=-1, keepdims=True))
    return here / jnp.sum(here * count, axis=-1, keepdims=True)


def student_kernel(
    normed, w_own_far, w_oth_far, ms_far, s_out_far, s_oth_far, zlocal, plocal, ccol, crow,
    own_far, oth_far, shares_own_far, shares_oth_far, zs, pooled, heads,
    w_own, w_oth, ms, s_out, s_oth, sems, own, oth, shares_own, shares_oth, out_sems,
):
    copies = begin((w_own_far, w_oth_far, ms_far, s_out_far, s_oth_far), (w_own, w_oth, ms, s_out, s_oth), sems)
    mask = same_patch()
    tokens = normed[...].reshape(TILES * ROWS, D)
    leaving = []
    sides = ((w_own, own, shares_own, own_far, shares_own_far), (w_oth, oth, shares_oth, oth_far, shares_oth_far))
    for head, (weight, keep, shares, keep_far, shares_far) in enumerate(sides):
        copies[head].wait()
        flat = mm(tokens, weight[...], NT)
        summed = jnp.zeros((CLIPS, HS), F32)
        for tile in range(TILES):
            query, key, value = split_qkv(flat[tile * ROWS : (tile + 1) * ROWS])
            keep[0, tile] = query
            keep[1, tile] = key
            keep[2, tile] = value
            scores = mm(query, key, NT) * SCALE + mask
            totals = []
            for clip in range(CLIPS):
                count = ccol[clip : clip + 1, :]
                share = clip_shares(scores, count)
                shares[tile, clip] = share
                share = share.astype(BF16).astype(F32) * crow[:, clip : clip + 1]
                totals.append(jnp.sum(share, axis=0, keepdims=True) * count)
            summed = summed + mm3(jnp.concatenate(totals, axis=0), value)
        leaving += begin((keep, shares), (keep_far, shares_far), out_sems.at[pl.ds(2 * head, 2)])
        heads[head] = summed / NTOK
    for copy in copies[2:]:
        copy.wait()
    zs[...] = mmh(heads[0], ms[0]) + mmh(heads[1], ms[1]) + zlocal[...]
    pooled[...] = mm3(heads[0], s_out[...]) + mm3(heads[1], s_oth[...]) + plocal[...]
    for copy in leaving:
        copy.wait()


def flip_kernel(normed_far, normed_oth_far, out_own_far, out_oth_far, half, half_oth, sems, out_own, out_oth, out_sems):
    copies = begin((normed_far, normed_oth_far), (half, half_oth), sems)
    leaving = []
    for index, (held, out, far) in enumerate(((half, out_own, out_own_far), (half_oth, out_oth, out_oth_far))):
        copies[index].wait()
        out[...] = jnp.transpose(held[...].reshape(TILES * ROWS, D))
        leaving += begin((out,), (far,), out_sems.at[pl.ds(index, 1)])
    for copy in leaving:
        copy.wait()


def message_kernel(frame, zs, ztc, pooled, heads, out):
    me = frame[0]
    zt = jnp.sum(ztc[...], axis=0)
    for peer in range(FRAMES):
        out[peer, 0:4, :] = zs[:, 0:128]
        out[peer, 4:8, :] = zs[:, 128:256]
        out[peer, 8:9, :] = zt[:, 0:128]
        out[peer, 9:10, :] = zt[:, 128:256]
        out[peer, 10:MSG, :] = jnp.zeros((MSG - 10, 128), F32)
        out[peer, 10:14, 0:HS] = pooled[:, peer * HS : (peer + 1) * HS]
        mine = (me == peer).astype(F32)
        partner = (jnp.bitwise_xor(me, 1) == peer).astype(F32)
        out[peer, 14:18, 0:HS] = heads[0] * mine + heads[1] * partner


def logits_kernel(got, protos, center, out, zs, heads):
    total = got[0]
    for source in range(1, FRAMES):
        total = total + got[source]
    z_s = jnp.concatenate([total[0:4], total[4:8]], axis=1)
    z_t = jnp.concatenate([total[8:9], total[9:10]], axis=1)
    zs[...] = z_s
    heads[...] = total[14:18, 0:HS]
    z_all = jnp.concatenate([z_s, z_t], axis=0)
    unit = z_all * rsqrt(jnp.sum(z_all * z_all, axis=-1, keepdims=True) + 1e-06)
    wide = mm3(unit, protos[...])
    logits = jnp.concatenate([wide[0:4] / TAU_STUD, (wide[4:5] - center[...]) / TAU_TEACH], axis=0)
    top = jnp.max(logits, axis=-1, keepdims=True)
    grown = jnp.exp(logits - top)
    size = jnp.sum(grown, axis=-1, keepdims=True)
    vec = mm3(grown, protos[...], NT)
    lane = lax.broadcasted_iota(jnp.int32, (5, 128), 1)
    tops = jnp.where(lane == 0, top, jnp.where(lane == 1, size, 0.0))
    for peer in range(FRAMES):
        out[peer, 0:5, :] = vec[:, 0:128]
        out[peer, 5:10, :] = vec[:, 128:256]
        out[peer, 10:15, :] = tops
        out[peer, 15:19, :] = total[10:14]
        out[peer, 19:MSG, :] = jnp.zeros((MSG - 19, 128), F32)


def code_of(peak):
    return jnp.ceil(jnp.log(jnp.maximum(peak, 1e-30)) * (STEP / math.log(2.0))) + 1.0


def scale_of(code):
    return jnp.exp(code * (math.log(2.0) / STEP))


def whole_max(x):
    return jnp.max(jnp.max(x, axis=-1, keepdims=True), axis=0, keepdims=True)


def stack3(parts):
    return jnp.concatenate([piece for part in parts for piece in pieces(part)], axis=0)


def back_kernel(
    peers, got, zs, heads, ms, own_far, oth_far, shares_own_far, shares_oth_far,
    ccol, crow, flip_own_far, flip_oth_far, out_far,
    keep_own, shares_own, keep_oth, shares_oth, flip, sems, out, out_sems, grad, rhs, last, line,
):
    count = TILES * ROWS
    copies = begin(
        (own_far, shares_own_far, oth_far, shares_oth_far, flip_own_far, flip_oth_far),
        (keep_own, shares_own, keep_oth, shares_oth, flip.at[:, pl.ds(0, count)], flip.at[:, pl.ds(count, count)]),
        sems,
    )
    tops = [got[source, 10:15, 0:1] for source in range(FRAMES)]
    top = functools.reduce(jnp.maximum, tops)
    size = jnp.zeros((5, 1), F32)
    low = jnp.zeros((5, 128), F32)
    high = jnp.zeros((5, 128), F32)
    for source in range(FRAMES):
        factor = jnp.exp(tops[source] - top)
        size = size + got[source, 10:15, 1:2] * factor
        low = low + got[source, 0:5, :] * factor
        high = high + got[source, 5:10, :] * factor
    expect = jnp.concatenate([low, high], axis=1) / size
    d_unit = (expect[0:4] - expect[4:5]) / (ALL_CLIPS * TAU_STUD)
    z_s = zs[...]
    inverse = rsqrt(jnp.sum(z_s * z_s, axis=-1, keepdims=True) + 1e-06)
    unit = z_s * inverse
    d_z = (d_unit - unit * jnp.sum(unit * d_unit, axis=-1, keepdims=True)) * inverse
    d_heads = mmh(d_z, ms[0], NT) / NTOK
    lane = lax.broadcasted_iota(jnp.int32, (ROWS, ROWS), 1)
    for half, (keep, shares) in enumerate(((keep_own, shares_own), (keep_oth, shares_oth))):
        copies[2 * half].wait()
        copies[2 * half + 1].wait()
        for tile in range(TILES):
            d_weights = mm3(d_heads, keep[2, tile], NT).astype(BF16).astype(F32)
            taken = [
                jnp.sum(shares[tile, clip].astype(BF16).astype(F32) * crow[:, clip : clip + 1], axis=0, keepdims=True)
                for clip in range(CLIPS)
            ]
            d_down = jnp.transpose(jnp.concatenate([d_weights] + taken, axis=0))
            inner = jnp.zeros((ROWS, ROWS), F32)
            grow_q = []
            for clip in range(CLIPS):
                share = shares[tile, clip] * ccol[clip : clip + 1, :]
                d_w = d_weights[clip : clip + 1, :]
                mean = jnp.sum(share * d_w, axis=-1, keepdims=True)
                inner = jnp.where(lane == clip, mean, inner)
                grow_q.append(share * (d_w - mean) * SCALE)
            inner = jnp.transpose(inner)
            grow_k = [
                jnp.transpose(shares[tile, clip])
                * ccol[clip : clip + 1, :]
                * (d_down[:, clip : clip + 1] - inner[clip : clip + 1, :])
                * SCALE
                for clip in range(CLIPS)
            ]
            wide_q = mm(stack3(grow_q), keep[1, tile])
            wide_k = mm(stack3(grow_k), keep[0, tile])
            totals = [jnp.zeros((ROWS, HS), F32) for _ in range(3)]
            for clip in range(CLIPS):
                many = crow[:, clip : clip + 1]
                first = 3 * clip * ROWS
                parts = [
                    wide[first : first + ROWS] + (wide[first + ROWS : first + 2 * ROWS] + wide[first + 2 * ROWS : first + 3 * ROWS])
                    for wide in (wide_q, wide_k)
                ]
                parts.append(d_down[:, CLIPS + clip : CLIPS + clip + 1] * d_heads[clip : clip + 1, :])
                totals = [total + many * part.astype(BF16).astype(F32) for total, part in zip(totals, parts)]
            packed = jnp.concatenate(totals, axis=1)
            first = packed.astype(BF16)
            second = (packed - first.astype(F32)).astype(BF16)
            rows = pl.ds((half * TILES + tile) * ROWS, ROWS)
            rhs[rows, 0:256] = first[:, 0:256]
            rhs[rows, 256:512] = second[:, 0:256]
            rhs[rows, 512:528] = jnp.concatenate([first[:, 256:264], second[:, 256:264]], axis=1)
    copies[4].wait()
    copies[5].wait()
    wide = mm(flip[...], rhs[...])
    main = wide[:, 0:256] + wide[:, 256:512]
    thin = jnp.transpose(wide[:, 512:520] + wide[:, 520:528])
    code = code_of(jnp.max(jnp.abs(main), axis=0, keepdims=True))
    grad[...] = jnp.round(main * (32000.0 / scale_of(code)))
    code_thin = code_of(jnp.max(jnp.abs(thin), axis=-1, keepdims=True))
    last[...] = jnp.round(thin * (32000.0 / scale_of(code_thin)))
    code_z = code_of(whole_max(jnp.abs(d_z)))
    sent_z = jnp.round(d_z * (32000.0 / scale_of(code_z)))
    mine = heads[...]
    code_h = code_of(whole_max(jnp.abs(mine)))
    sent_h = jnp.round(mine * (32000.0 / scale_of(code_h)))
    pooled = jnp.concatenate([got[source, 15:19, 0:HS] for source in range(FRAMES)], axis=1)
    code_p = code_of(whole_max(jnp.abs(pooled)))
    sent_p = jnp.round(pooled * (32000.0 / scale_of(code_p)))
    lane = lax.broadcasted_iota(jnp.int32, (1, 128), 1)
    codes = jnp.where(lane == 64, code_z, jnp.where(lane == 65, code_h, jnp.where(lane == 66, code_p, 0.0)))
    block = D // peers
    line[...] = jnp.zeros((QROWS, 256), F32)
    line[44:48, :] = sent_z
    line[48:49, 0:HS] = sent_h[0:1]
    line[48:49, 128 : 128 + HS] = sent_h[1:2]
    line[49:50, 0:HS] = sent_h[2:3]
    line[49:50, 128 : 128 + HS] = sent_h[3:4]
    line[55:56, :] = code
    leaving = []
    for peer in range(peers):
        line[0:block, :] = grad[peer * block : (peer + 1) * block, :]
        part = sent_p[:, peer * block : (peer + 1) * block]
        line[50:54, 0:block] = part
        thin_part = last[:, peer * block : (peer + 1) * block]
        line[50:54, 64 : 64 + block] = thin_part[0:4]
        line[50:54, 128 : 128 + block] = thin_part[4:8]
        line[50:54, 192:193] = code_thin[0:4]
        line[50:54, 193:194] = code_thin[4:8]
        line[54:55, 0:128] = codes
        out[peer] = line[...].astype(jnp.int32).astype(jnp.int16)
        leaving += begin((out.at[peer],), (out_far.at[peer],), out_sems.at[pl.ds(peer, 1)])
    for copy in leaving:
        copy.wait()


def final_kernel(peers, got, bottle, g_qkv, g_out, g_bottle, z_all, h_all, p_all):
    block = D // peers
    main = jnp.zeros((block, 256), F32)
    thin_a = jnp.zeros((4, block), F32)
    thin_b = jnp.zeros((4, block), F32)
    for source in range(peers):
        line = got[source].astype(jnp.int32).astype(F32)
        main = main + line[0:block] * (scale_of(line[55:56]) / 32000.0)
        thin_a = thin_a + line[50:54, 64 : 64 + block] * (scale_of(line[50:54, 192:193]) / 32000.0)
        thin_b = thin_b + line[50:54, 128 : 128 + block] * (scale_of(line[50:54, 193:194]) / 32000.0)
        scales = scale_of(line[54:55, 0:128]) / 32000.0
        first = source * CLIPS
        z_all[first : first + 4, :] = line[44:48] * scales[:, 64:65]
        scale_h = scales[:, 65:66]
        h_all[first : first + 1, :] = line[48:49, 0:HS] * scale_h
        h_all[first + 1 : first + 2, :] = line[48:49, 128 : 128 + HS] * scale_h
        h_all[first + 2 : first + 3, :] = line[49:50, 0:HS] * scale_h
        h_all[first + 3 : first + 4, :] = line[49:50, 128 : 128 + HS] * scale_h
        p_all[first : first + 4, :] = line[50:54, 0:block] * scales[:, 66:67]
    g_qkv[:, 0:256] = main
    g_qkv[:, 256:264] = jnp.transpose(jnp.concatenate([thin_a, thin_b], axis=0))
    d_z = z_all[...]
    g_bottle[...] = mmh(p_all[...], d_z, TN)
    g_out[...] = mmh(bottle[...].astype(F32), mmh(h_all[...], d_z, TN), NT)


def local(
    global_clips,
    frame_map,
    teacher_qkv,
    teacher_out,
    teacher_bottle,
    student_qkv,
    student_out,
    student_bottle,
    prototypes,
    center,
):
    frame = lax.axis_index("frame")
    peers = lax.axis_size("crop") * lax.axis_size("dp")
    crops = lax.axis_size("crop")
    swap = [(index, index ^ 1) for index in range(FRAMES)]
    tokens = global_clips[0, 0]
    (spread,) = call(
        spread_kernel,
        [((FRAMES, tokens.shape[0] // 2, D), BF16)],
        tokens,
    )
    mixed = lax.all_to_all(spread, "frame", 0, 0, tiled=True)
    t_own = teacher_qkv.T
    s_own = student_qkv.T
    t_oth = lax.ppermute(t_own, "frame", swap)
    s_oth = lax.ppermute(s_own, "frame", swap)
    t_out_oth = lax.ppermute(teacher_out, "frame", swap)
    s_out_oth = lax.ppermute(student_out, "frame", swap)
    mt, ms, otz, zlocal, plocal, ccol, crow = call(
        prep_kernel,
        [
            ((2, HS, BOTTLE), F32),
            ((2, HS, BOTTLE), F32),
            ((1, BOTTLE), F32),
            ((CLIPS, BOTTLE), F32),
            ((CLIPS, D), F32),
            ((CLIPS, ROWS), F32),
            ((ROWS, ROWS), F32),
        ],
        frame_map[0], frame.astype(jnp.int32).reshape(1),
        tokens, teacher_out, t_out_oth, student_out, s_out_oth, teacher_bottle, student_bottle,
        smem=2,
    )
    normed, zt = call(
        teacher_kernel,
        [((TILES, ROWS, D), BF16), ((crops, 1, BOTTLE), F32)],
        mixed, t_own, t_oth, mt, otz,
        hbm_in=(1, 2, 3), scratch=room(t_own, t_oth, mt),
    )
    ztc = lax.all_to_all(zt, "crop", 0, 0, tiled=True)
    keep = jax.ShapeDtypeStruct((3, TILES, ROWS, HS), BF16)
    table = jax.ShapeDtypeStruct((TILES, CLIPS, ROWS, ROWS), F32)
    own, oth, shares_own, shares_oth, zs, pooled, heads = call(
        student_kernel,
        [
            (keep.shape, BF16),
            (keep.shape, BF16),
            (table.shape, F32),
            (table.shape, F32),
            ((CLIPS, BOTTLE), F32),
            ((CLIPS, D), F32),
            ((2, CLIPS, HS), F32),
        ],
        normed, s_own, s_oth, ms, student_out, s_out_oth, zlocal, plocal, ccol, crow,
        hbm_in=(1, 2, 3, 4, 5), hbm_out=(0, 1, 2, 3), limit=20,
        scratch=room(s_own, s_oth, ms, student_out, s_out_oth) + room(keep, keep, table, table),
    )
    (sent,) = call(
        message_kernel,
        [((FRAMES, MSG, 128), F32)],
        frame.astype(jnp.int32).reshape(1), zs, ztc, pooled, heads, smem=1,
    )
    sent, leaving = lax.optimization_barrier((sent, (normed, oth, shares_oth)))
    got = lax.all_to_all(sent, "frame", 0, 0, tiled=True)
    normed_oth = lax.ppermute(leaving[0], "frame", swap)
    shares_got = lax.ppermute(leaving[2], "frame", swap)
    kept_oth = lax.ppermute(leaving[1], "frame", swap)
    flat = jax.ShapeDtypeStruct((D, TILES * ROWS), BF16)
    flips = call(
        flip_kernel,
        [(flat.shape, BF16), (flat.shape, BF16)],
        normed, normed_oth,
        hbm_in=(0, 1), hbm_out=(0, 1), scratch=room(normed, normed_oth) + room(flat, flat),
    )
    sent, z_s, my_heads = call(
        logits_kernel,
        [((FRAMES, MSG, 128), F32), ((CLIPS, BOTTLE), F32), ((CLIPS, HS), F32)],
        got, prototypes, center.reshape(1, -1),
    )
    got = lax.all_to_all(sent, "frame", 0, 0, tiled=True)
    (sent,) = call(
        functools.partial(back_kernel, peers),
        [((peers, QROWS, 256), jnp.int16)],
        got, z_s, my_heads, ms, own, kept_oth, shares_own, shares_got, ccol, crow, flips[0], flips[1],
        hbm_in=(4, 5, 6, 7, 10, 11), hbm_out=(0,), limit=30,
        scratch=room(own, shares_own, kept_oth, shares_got)[:-1]
        + [
            pltpu.VMEM((D, 2 * TILES * ROWS), BF16),
            pltpu.SemaphoreType.DMA((6,)),
            pltpu.VMEM((peers, QROWS, 256), jnp.int16),
            pltpu.SemaphoreType.DMA((peers,)),
            pltpu.VMEM((D, 256), F32),
            pltpu.VMEM((2 * TILES * ROWS, 528), BF16),
            pltpu.VMEM((8, D), F32),
            pltpu.VMEM((QROWS, 256), F32),
        ],
    )
    got = lax.all_to_all(sent, ("crop", "dp"), 0, 0, tiled=True)
    block = D // peers
    place = lax.axis_index("crop") * lax.axis_size("dp") + lax.axis_index("dp")
    bottle = lax.dynamic_slice_in_dim(student_bottle, place * block, block, axis=0)
    g_qkv, g_out, g_bottle = call(
        functools.partial(final_kernel, peers),
        [((block, 3 * HS), F32), ((block, HS), F32), ((block, BOTTLE), F32)],
        got, bottle,
        scratch=[
            pltpu.VMEM((peers * CLIPS, BOTTLE), F32),
            pltpu.VMEM((peers * CLIPS, HS), F32),
            pltpu.VMEM((peers * CLIPS, block), F32),
        ],
    )
    return g_qkv, g_out.T, g_bottle


def solution(mesh):
    return program(mesh)


def program(mesh):
    return jax.shard_map(
        local,
        mesh=mesh,
        in_specs=(
            P("dp", "frame", "crop", None),
            P("dp", "crop", None),
            P(None, "frame"),
            P("frame", None),
            P(),
            P(None, "frame"),
            P("frame", None),
            P(),
            P(None, "frame"),
            P("frame"),
        ),
        out_specs=(P(("crop", "dp"), "frame"), P("frame", ("crop", "dp")), P(("crop", "dp"), None)),
        check_vma=False,
    )
```

```python
import functools
import math

import jax
import jax.numpy as jnp
from jax import lax
from jax.experimental import pallas as pl
from jax.experimental.pallas import tpu as pltpu
from jax.sharding import PartitionSpec as P


D = 1408
HS = 88
FRAMES = 16
BOTTLE = 256
GP = 8
ROWS = FRAMES * GP
TILES = 4
LFRAMES = 8
QKV = 3 * HS
PITCH = 272
CLIPS = 4
NTOK = 512
NTEACH = 4096
TAU_TEACH = 0.04
TAU_STUD = 0.1
ALL_CLIPS = 16
HIGH = lax.Precision.HIGHEST
F32 = jnp.float32
BF16 = jnp.bfloat16
NEG = -1e30
SCALE = 1.0 / math.sqrt(HS)
MSG = 24
QROWS = 56
STEP = 64.0
INTERPRET = False

NN = (((1,), (0,)), ((), ()))
NT = (((1,), (1,)), ((), ()))
TN = (((0,), (0,)), ((), ()))


def call(kernel, outs, *args, scratch=(), smem=0, hbm_in=(), hbm_out=(), limit=16):
    def space(index, in_hbm):
        return pl.BlockSpec(memory_space=pltpu.HBM if index in in_hbm else pltpu.VMEM)

    spec = [pl.BlockSpec(memory_space=pltpu.SMEM)] * smem
    spec += [space(index, hbm_in) for index in range(smem, len(args))]
    args = [pltpu.with_memory_space_constraint(arg, pltpu.HBM) if index in hbm_in else arg for index, arg in enumerate(args)]
    return pl.pallas_call(
        kernel,
        out_shape=tuple(
            pltpu.HBM(shape, dtype) if index in hbm_out else jax.ShapeDtypeStruct(shape, dtype)
            for index, (shape, dtype) in enumerate(outs)
        ),
        in_specs=spec,
        out_specs=tuple(space(index, hbm_out) for index in range(len(outs))),
        scratch_shapes=list(scratch),
        compiler_params=pltpu.CompilerParams(vmem_limit_bytes=limit * 2**20),
        interpret=INTERPRET,
    )(*args)


def room(*arrays):
    held = [pltpu.VMEM(tuple(array.shape), array.dtype) for array in arrays]
    return held + [pltpu.SemaphoreType.DMA((len(held),))]


def begin(sources, targets, sems):
    copies = [pltpu.make_async_copy(source, target, sems.at[i]) for i, (source, target) in enumerate(zip(sources, targets))]
    for copy in copies:
        copy.start()
    return copies


def mm(a, b, dims=NN):
    return lax.dot_general(a, b, dims, preferred_element_type=F32)


def mmh(a, b, dims=NN):
    return lax.dot_general(a, b, dims, precision=HIGH, preferred_element_type=F32)


def pieces(x):
    top = x.astype(BF16)
    rest = x - top.astype(F32)
    mid = rest.astype(BF16)
    return top, mid, (rest - mid.astype(F32)).astype(BF16)


def mm3(x, y, dims=NN):
    top, mid, low = pieces(x)
    return mm(top, y, dims) + (mm(mid, y, dims) + mm(low, y, dims))


def rsqrt(x):
    guess = lax.rsqrt(x)
    return guess * (1.5 - 0.5 * x * guess * guess)


def same_patch():
    row = lax.broadcasted_iota(jnp.int32, (ROWS, ROWS), 0)
    col = lax.broadcasted_iota(jnp.int32, (ROWS, ROWS), 1)
    return jnp.where((row % GP) == (col % GP), 0.0, NEG).astype(F32)


def split_qkv(flat, tile, head):
    rows = flat[tile * ROWS : (tile + 1) * ROWS]
    return [rows[:, head * PITCH + part * HS : head * PITCH + (part + 1) * HS].astype(BF16) for part in range(3)]


def spread_kernel(tok, out):
    half = out.shape[1]
    for peer in range(FRAMES):
        out[peer] = tok[(peer % 2) * half : (peer % 2 + 1) * half, :]


def prep_kernel(
    maps, frame, tok, t_out, t_oth, s_out, s_oth, t_bot, s_bot, mt, ms, otz, zlocal, plocal, ccol, crow
):
    total = jnp.sum(tok[...].astype(F32), axis=0, keepdims=True)
    otz[...] = mm3(total, t_bot[...])
    osz = mm3(total, s_bot[...])
    mt[0] = mm(t_out[...], t_bot[...])
    mt[1] = mm(t_oth[...], t_bot[...])
    ms[0] = mm(s_out[...], s_bot[...])
    ms[1] = mm(s_oth[...], s_bot[...])
    lane = lax.broadcasted_iota(jnp.int32, (1, ROWS), 1)
    row = lax.broadcasted_iota(jnp.int32, (ROWS, ROWS), 0) // GP
    down = [jnp.zeros((ROWS, ROWS), F32) for _ in range(CLIPS)]
    across = [jnp.zeros((1, ROWS), F32) for _ in range(CLIPS)]
    mine = [jnp.zeros((1, ROWS), F32) for _ in range(CLIPS)]
    for step in range(LFRAMES):
        for clip in range(CLIPS):
            index = maps[clip, step]
            down[clip] = down[clip] + jnp.where(row == index, 1.0, 0.0)
            across[clip] = across[clip] + jnp.where(lane // GP == index, 1.0, 0.0)
            mine[clip] = mine[clip] + jnp.where(index == frame[0], 1.0, 0.0)
    for clip in range(CLIPS):
        crow[clip] = down[clip]
        ccol[clip : clip + 1, :] = across[clip]
        frac = mine[clip][:, 0:1] / NTOK
        zlocal[clip : clip + 1, :] = frac * osz
        plocal[clip : clip + 1, :] = frac * total


def teacher_kernel(x, w_own_far, w_oth_far, mt_far, otz, normed, zt, weights, mt, sems):
    copies = begin((w_own_far, w_oth_far, mt_far), (weights.at[pl.ds(0, QKV)], weights.at[pl.ds(PITCH, QKV)], mt), sems)
    for group in range(2):
        values = x[:, group * 2 * GP : (group + 1) * 2 * GP, :].astype(F32)
        middle = jnp.mean(values, axis=-1, keepdims=True)
        moved = values - middle
        spread = jnp.mean(moved * moved, axis=-1, keepdims=True)
        token = moved * rsqrt(spread + 1e-06)
        normed[2 * group] = token[:, :GP].reshape(ROWS, D).astype(BF16)
        normed[2 * group + 1] = token[:, GP:].reshape(ROWS, D).astype(BF16)
    mask = same_patch()
    tokens = normed[...].reshape(TILES * ROWS, D)
    total = otz[...]
    for copy in copies:
        copy.wait()
    flat = mm(tokens, weights[...], NT)
    ones = jnp.ones((8, ROWS), BF16)
    for head in range(2):
        summed = jnp.zeros((8, HS), F32)
        for tile in range(TILES):
            query, key, value = split_qkv(flat, tile, head)
            scores = mm(key, query, NT) * SCALE + mask
            scores = jnp.exp(scores - jnp.max(scores, axis=0, keepdims=True))
            share = scores / jnp.sum(scores, axis=0, keepdims=True)
            received = mm(ones, share.astype(BF16), NT)
            summed = summed + mm3(received, value)
        total = total + mmh(summed[0:1], mt[head])
    for crop in range(zt.shape[0]):
        zt[crop] = total / NTEACH


def clip_shares(scores, count):
    here = jnp.where(count > 0.0, scores, NEG)
    here = jnp.exp(here - jnp.max(here, axis=0, keepdims=True))
    return here / jnp.sum(here * count, axis=0, keepdims=True)


def student_kernel(
    normed, w_own_far, w_oth_far, ms_far, s_out_far, s_oth_far, zlocal, plocal, ccol, crow,
    own_far, oth_far, shares_own_far, shares_oth_far, zs, pooled, heads,
    weights, ms, s_out, s_oth, sems, own, oth, shares_own, shares_oth, out_sems,
):
    copies = begin(
        (w_own_far, w_oth_far, ms_far, s_out_far, s_oth_far),
        (weights.at[pl.ds(0, QKV)], weights.at[pl.ds(PITCH, QKV)], ms, s_out, s_oth),
        sems,
    )
    mask = same_patch()
    tokens = normed[...].reshape(TILES * ROWS, D)
    leaving = []
    copies[0].wait()
    copies[1].wait()
    flat = mm(tokens, weights[...], NT)
    counts = jnp.concatenate([ccol[...], ccol[...]], axis=0).astype(BF16)
    sides = ((own, shares_own, own_far, shares_own_far), (oth, shares_oth, oth_far, shares_oth_far))
    for head, (keep, shares, keep_far, shares_far) in enumerate(sides):
        summed = jnp.zeros((CLIPS, HS), F32)
        for tile in range(TILES):
            query, key, value = split_qkv(flat, tile, head)
            keep[0, tile] = query
            keep[1, tile] = key
            keep[2, tile] = value
            scores = mm(key, query, NT) * SCALE + mask
            totals = []
            for clip in range(CLIPS):
                share = clip_shares(scores, crow[clip])
                shares[tile, clip, 0:ROWS, :] = share
                received = mm(counts, share.astype(BF16), NT)[clip : clip + 1]
                shares[tile, clip, ROWS : ROWS + 1, :] = received
                totals.append(received * ccol[clip : clip + 1, :])
            summed = summed + mm3(jnp.concatenate(totals, axis=0), value)
        leaving += begin((keep, shares), (keep_far, shares_far), out_sems.at[pl.ds(2 * head, 2)])
        heads[head] = summed / NTOK
    for copy in copies[2:]:
        copy.wait()
    zs[...] = mmh(heads[0], ms[0]) + mmh(heads[1], ms[1]) + zlocal[...]
    pooled[...] = mm3(heads[0], s_out[...]) + mm3(heads[1], s_oth[...]) + plocal[...]
    for copy in leaving:
        copy.wait()


def flip_kernel(normed_far, normed_oth_far, out_own_far, out_oth_far, half, half_oth, sems, out_own, out_oth, out_sems):
    copies = begin((normed_far, normed_oth_far), (half, half_oth), sems)
    leaving = []
    for index, (held, out, far) in enumerate(((half, out_own, out_own_far), (half_oth, out_oth, out_oth_far))):
        copies[index].wait()
        out[...] = jnp.transpose(held[...].reshape(TILES * ROWS, D))
        leaving += begin((out,), (far,), out_sems.at[pl.ds(index, 1)])
    for copy in leaving:
        copy.wait()


def message_kernel(frame, zs, ztc, pooled, heads, out):
    me = frame[0]
    zt = jnp.sum(ztc[...], axis=0)
    for peer in range(FRAMES):
        out[peer, 0:4, :] = zs[:, 0:128]
        out[peer, 4:8, :] = zs[:, 128:256]
        out[peer, 8:9, :] = zt[:, 0:128]
        out[peer, 9:10, :] = zt[:, 128:256]
        out[peer, 10:MSG, :] = jnp.zeros((MSG - 10, 128), F32)
        out[peer, 10:14, 0:HS] = pooled[:, peer * HS : (peer + 1) * HS]
        mine = (me == peer).astype(F32)
        partner = (jnp.bitwise_xor(me, 1) == peer).astype(F32)
        out[peer, 14:18, 0:HS] = heads[0] * mine + heads[1] * partner


def logits_kernel(got, protos, center, out, zs, heads):
    total = got[0]
    for source in range(1, FRAMES):
        total = total + got[source]
    z_s = jnp.concatenate([total[0:4], total[4:8]], axis=1)
    z_t = jnp.concatenate([total[8:9], total[9:10]], axis=1)
    zs[...] = z_s
    heads[...] = total[14:18, 0:HS]
    z_all = jnp.concatenate([z_s, z_t], axis=0)
    unit = z_all * rsqrt(jnp.sum(z_all * z_all, axis=-1, keepdims=True) + 1e-06)
    wide = mm3(unit, protos[...])
    logits = jnp.concatenate([wide[0:4] / TAU_STUD, (wide[4:5] - center[...]) / TAU_TEACH], axis=0)
    top = jnp.max(logits, axis=-1, keepdims=True)
    grown = jnp.exp(logits - top)
    size = jnp.sum(grown, axis=-1, keepdims=True)
    vec = mm3(grown, protos[...], NT)
    lane = lax.broadcasted_iota(jnp.int32, (5, 128), 1)
    tops = jnp.where(lane == 0, top, jnp.where(lane == 1, size, 0.0))
    for peer in range(FRAMES):
        out[peer, 0:5, :] = vec[:, 0:128]
        out[peer, 5:10, :] = vec[:, 128:256]
        out[peer, 10:15, :] = tops
        out[peer, 15:19, :] = total[10:14]
        out[peer, 19:MSG, :] = jnp.zeros((MSG - 19, 128), F32)


def code_of(peak):
    return jnp.ceil(jnp.log(jnp.maximum(peak, 1e-30)) * (STEP / math.log(2.0))) + 1.0


def scale_of(code):
    return jnp.exp(code * (math.log(2.0) / STEP))


def whole_max(x):
    return jnp.max(jnp.max(x, axis=-1, keepdims=True), axis=0, keepdims=True)


def stack2(parts):
    return jnp.concatenate([piece for part in parts for piece in pieces(part)[:2]], axis=0)


def back_kernel(
    peers, got, zs, heads, ms, own_far, oth_far, shares_own_far, shares_oth_far,
    ccol, crow, flip_own_far, flip_oth_far, out_far,
    keep_own, shares_own, keep_oth, shares_oth, flip, sems, out, out_sems, grad, rhs, last, line,
):
    count = TILES * ROWS
    copies = begin(
        (own_far, shares_own_far, oth_far, shares_oth_far, flip_own_far, flip_oth_far),
        (keep_own, shares_own, keep_oth, shares_oth, flip.at[:, pl.ds(0, count)], flip.at[:, pl.ds(count, count)]),
        sems,
    )
    tops = [got[source, 10:15, 0:1] for source in range(FRAMES)]
    top = functools.reduce(jnp.maximum, tops)
    size = jnp.zeros((5, 1), F32)
    low = jnp.zeros((5, 128), F32)
    high = jnp.zeros((5, 128), F32)
    for source in range(FRAMES):
        factor = jnp.exp(tops[source] - top)
        size = size + got[source, 10:15, 1:2] * factor
        low = low + got[source, 0:5, :] * factor
        high = high + got[source, 5:10, :] * factor
    expect = jnp.concatenate([low, high], axis=1) / size
    d_unit = (expect[0:4] - expect[4:5]) / (ALL_CLIPS * TAU_STUD)
    z_s = zs[...]
    inverse = rsqrt(jnp.sum(z_s * z_s, axis=-1, keepdims=True) + 1e-06)
    unit = z_s * inverse
    d_z = (d_unit - unit * jnp.sum(unit * d_unit, axis=-1, keepdims=True)) * inverse
    d_heads = mmh(d_z, ms[0], NT) / NTOK
    for half, (keep, shares) in enumerate(((keep_own, shares_own), (keep_oth, shares_oth))):
        copies[2 * half].wait()
        copies[2 * half + 1].wait()
        for tile in range(TILES):
            d_weights = mm3(d_heads, keep[2, tile], NT).astype(BF16).astype(F32)
            d_weights = d_weights * SCALE
            taken = [shares[tile, clip, ROWS : ROWS + 1, :] for clip in range(CLIPS)]
            d_down = jnp.transpose(jnp.concatenate([d_weights] + taken, axis=0))
            grow_q, grow_k = [], []
            for clip in range(CLIPS):
                count = ccol[clip : clip + 1, :]
                share = shares[tile, clip, 0:ROWS, :]
                d_w = jnp.broadcast_to(d_down[:, clip : clip + 1], (ROWS, ROWS))
                mean = jnp.sum(share * (crow[clip] * d_w), axis=0, keepdims=True)
                base = share * (d_w - mean)
                grow_k.append(base * count)
                grow_q.append(jnp.transpose(base) * count)
            wide_q = mm(stack2(grow_q), keep[1, tile])
            wide_k = mm(stack2(grow_k), keep[0, tile])
            totals = [jnp.zeros((ROWS, HS), F32) for _ in range(3)]
            for clip in range(CLIPS):
                many = crow[clip, :, 0:HS]
                first = 2 * clip * ROWS
                parts = [wide[first : first + ROWS] + wide[first + ROWS : first + 2 * ROWS] for wide in (wide_q, wide_k)]
                parts.append(d_down[:, CLIPS + clip : CLIPS + clip + 1] * d_heads[clip : clip + 1, :])
                totals = [total + many * part.astype(BF16).astype(F32) for total, part in zip(totals, parts)]
            packed = jnp.concatenate(totals, axis=1)
            first = packed.astype(BF16)
            second = (packed - first.astype(F32)).astype(BF16)
            rows = pl.ds((half * TILES + tile) * ROWS, ROWS)
            rhs[rows, 0:256] = first[:, 0:256]
            rhs[rows, 256:512] = second[:, 0:256]
            rhs[rows, 512:528] = jnp.concatenate([first[:, 256:264], second[:, 256:264]], axis=1)
    copies[4].wait()
    copies[5].wait()
    wide = mm(flip[...], rhs[...])
    main = wide[:, 0:256] + wide[:, 256:512]
    thin = jnp.transpose(wide[:, 512:520] + wide[:, 520:528])
    code = code_of(jnp.max(jnp.abs(main), axis=0, keepdims=True))
    grad[...] = jnp.round(main * (32000.0 / scale_of(code)))
    code_thin = code_of(jnp.max(jnp.abs(thin), axis=-1, keepdims=True))
    last[...] = jnp.round(thin * (32000.0 / scale_of(code_thin)))
    code_z = code_of(whole_max(jnp.abs(d_z)))
    sent_z = jnp.round(d_z * (32000.0 / scale_of(code_z)))
    mine = heads[...]
    code_h = code_of(whole_max(jnp.abs(mine)))
    sent_h = jnp.round(mine * (32000.0 / scale_of(code_h)))
    pooled = jnp.concatenate([got[source, 15:19, 0:HS] for source in range(FRAMES)], axis=1)
    code_p = code_of(whole_max(jnp.abs(pooled)))
    sent_p = jnp.round(pooled * (32000.0 / scale_of(code_p)))
    lane = lax.broadcasted_iota(jnp.int32, (1, 128), 1)
    codes = jnp.where(lane == 64, code_z, jnp.where(lane == 65, code_h, jnp.where(lane == 66, code_p, 0.0)))
    block = D // peers
    line[...] = jnp.zeros((QROWS, 256), F32)
    line[44:48, :] = sent_z
    line[48:49, 0:HS] = sent_h[0:1]
    line[48:49, 128 : 128 + HS] = sent_h[1:2]
    line[49:50, 0:HS] = sent_h[2:3]
    line[49:50, 128 : 128 + HS] = sent_h[3:4]
    line[55:56, :] = code
    leaving = []
    for peer in range(peers):
        line[0:block, :] = grad[peer * block : (peer + 1) * block, :]
        part = sent_p[:, peer * block : (peer + 1) * block]
        line[50:54, 0:block] = part
        thin_part = last[:, peer * block : (peer + 1) * block]
        line[50:54, 64 : 64 + block] = thin_part[0:4]
        line[50:54, 128 : 128 + block] = thin_part[4:8]
        line[50:54, 192:193] = code_thin[0:4]
        line[50:54, 193:194] = code_thin[4:8]
        line[54:55, 0:128] = codes
        out[peer] = line[...].astype(jnp.int32).astype(jnp.int16)
        leaving += begin((out.at[peer],), (out_far.at[peer],), out_sems.at[pl.ds(peer, 1)])
    for copy in leaving:
        copy.wait()


def final_kernel(peers, got, bottle, g_qkv, g_out, g_bottle, z_all, h_all, p_all):
    block = D // peers
    main = jnp.zeros((block, 256), F32)
    thin_a = jnp.zeros((4, block), F32)
    thin_b = jnp.zeros((4, block), F32)
    for source in range(peers):
        line = got[source].astype(jnp.int32).astype(F32)
        main = main + line[0:block] * (scale_of(line[55:56]) / 32000.0)
        thin_a = thin_a + line[50:54, 64 : 64 + block] * (scale_of(line[50:54, 192:193]) / 32000.0)
        thin_b = thin_b + line[50:54, 128 : 128 + block] * (scale_of(line[50:54, 193:194]) / 32000.0)
        scales = scale_of(line[54:55, 0:128]) / 32000.0
        first = source * CLIPS
        z_all[first : first + 4, :] = line[44:48] * scales[:, 64:65]
        scale_h = scales[:, 65:66]
        h_all[first : first + 1, :] = line[48:49, 0:HS] * scale_h
        h_all[first + 1 : first + 2, :] = line[48:49, 128 : 128 + HS] * scale_h
        h_all[first + 2 : first + 3, :] = line[49:50, 0:HS] * scale_h
        h_all[first + 3 : first + 4, :] = line[49:50, 128 : 128 + HS] * scale_h
        p_all[first : first + 4, :] = line[50:54, 0:block] * scales[:, 66:67]
    g_qkv[:, 0:256] = main
    g_qkv[:, 256:264] = jnp.transpose(jnp.concatenate([thin_a, thin_b], axis=0))
    d_z = z_all[...]
    g_bottle[...] = mmh(p_all[...], d_z, TN)
    g_out[...] = mmh(bottle[...].astype(F32), mmh(h_all[...], d_z, TN), NT)


def local(
    global_clips,
    frame_map,
    teacher_qkv,
    teacher_out,
    teacher_bottle,
    student_qkv,
    student_out,
    student_bottle,
    prototypes,
    center,
):
    frame = lax.axis_index("frame")
    peers = lax.axis_size("crop") * lax.axis_size("dp")
    crops = lax.axis_size("crop")
    swap = [(index, index ^ 1) for index in range(FRAMES)]
    tokens = global_clips[0, 0]
    (spread,) = call(
        spread_kernel,
        [((FRAMES, tokens.shape[0] // 2, D), BF16)],
        tokens,
    )
    mixed = lax.all_to_all(spread, "frame", 0, 0, tiled=True)
    t_own = teacher_qkv.T
    s_own = student_qkv.T
    t_oth = lax.ppermute(t_own, "frame", swap)
    s_oth = lax.ppermute(s_own, "frame", swap)
    t_out_oth = lax.ppermute(teacher_out, "frame", swap)
    s_out_oth = lax.ppermute(student_out, "frame", swap)
    mt, ms, otz, zlocal, plocal, ccol, crow = call(
        prep_kernel,
        [
            ((2, HS, BOTTLE), F32),
            ((2, HS, BOTTLE), F32),
            ((1, BOTTLE), F32),
            ((CLIPS, BOTTLE), F32),
            ((CLIPS, D), F32),
            ((CLIPS, ROWS), F32),
            ((CLIPS, ROWS, ROWS), F32),
        ],
        frame_map[0], frame.astype(jnp.int32).reshape(1),
        tokens, teacher_out, t_out_oth, student_out, s_out_oth, teacher_bottle, student_bottle,
        smem=2,
    )
    normed, zt = call(
        teacher_kernel,
        [((TILES, ROWS, D), BF16), ((crops, 1, BOTTLE), F32)],
        mixed, t_own, t_oth, mt, otz,
        hbm_in=(1, 2, 3),
        scratch=[pltpu.VMEM((2 * PITCH, D), BF16), pltpu.VMEM(mt.shape, F32), pltpu.SemaphoreType.DMA((3,))],
    )
    ztc = lax.all_to_all(zt, "crop", 0, 0, tiled=True)
    keep = jax.ShapeDtypeStruct((3, TILES, ROWS, HS), BF16)
    table = jax.ShapeDtypeStruct((TILES, CLIPS, ROWS + 8, ROWS), F32)
    own, oth, shares_own, shares_oth, zs, pooled, heads = call(
        student_kernel,
        [
            (keep.shape, BF16),
            (keep.shape, BF16),
            (table.shape, F32),
            (table.shape, F32),
            ((CLIPS, BOTTLE), F32),
            ((CLIPS, D), F32),
            ((2, CLIPS, HS), F32),
        ],
        normed, s_own, s_oth, ms, student_out, s_out_oth, zlocal, plocal, ccol, crow,
        hbm_in=(1, 2, 3, 4, 5), hbm_out=(0, 1, 2, 3), limit=20,
        scratch=[pltpu.VMEM((2 * PITCH, D), BF16)]
        + room(ms, student_out, s_out_oth)[:-1]
        + [pltpu.SemaphoreType.DMA((5,))]
        + room(keep, keep, table, table),
    )
    (sent,) = call(
        message_kernel,
        [((FRAMES, MSG, 128), F32)],
        frame.astype(jnp.int32).reshape(1), zs, ztc, pooled, heads, smem=1,
    )
    sent, leaving = lax.optimization_barrier((sent, (normed, oth, shares_oth)))
    got = lax.all_to_all(sent, "frame", 0, 0, tiled=True)
    normed_oth = lax.ppermute(leaving[0], "frame", swap)
    shares_got = lax.ppermute(leaving[2], "frame", swap)
    kept_oth = lax.ppermute(leaving[1], "frame", swap)
    flat = jax.ShapeDtypeStruct((D, TILES * ROWS), BF16)
    flips = call(
        flip_kernel,
        [(flat.shape, BF16), (flat.shape, BF16)],
        normed, normed_oth,
        hbm_in=(0, 1), hbm_out=(0, 1), scratch=room(normed, normed_oth) + room(flat, flat),
    )
    sent, z_s, my_heads = call(
        logits_kernel,
        [((FRAMES, MSG, 128), F32), ((CLIPS, BOTTLE), F32), ((CLIPS, HS), F32)],
        got, prototypes, center.reshape(1, -1),
    )
    got = lax.all_to_all(sent, "frame", 0, 0, tiled=True)
    (sent,) = call(
        functools.partial(back_kernel, peers),
        [((peers, QROWS, 256), jnp.int16)],
        got, z_s, my_heads, ms, own, kept_oth, shares_own, shares_got, ccol, crow, flips[0], flips[1],
        hbm_in=(4, 5, 6, 7, 10, 11), hbm_out=(0,), limit=30,
        scratch=room(own, shares_own, kept_oth, shares_got)[:-1]
        + [
            pltpu.VMEM((D, 2 * TILES * ROWS), BF16),
            pltpu.SemaphoreType.DMA((6,)),
            pltpu.VMEM((peers, QROWS, 256), jnp.int16),
            pltpu.SemaphoreType.DMA((peers,)),
            pltpu.VMEM((D, 256), F32),
            pltpu.VMEM((2 * TILES * ROWS, 528), BF16),
            pltpu.VMEM((8, D), F32),
            pltpu.VMEM((QROWS, 256), F32),
        ],
    )
    got = lax.all_to_all(sent, ("crop", "dp"), 0, 0, tiled=True)
    block = D // peers
    place = lax.axis_index("crop") * lax.axis_size("dp") + lax.axis_index("dp")
    bottle = lax.dynamic_slice_in_dim(student_bottle, place * block, block, axis=0)
    g_qkv, g_out, g_bottle = call(
        functools.partial(final_kernel, peers),
        [((block, 3 * HS), F32), ((block, HS), F32), ((block, BOTTLE), F32)],
        got, bottle,
        scratch=[
            pltpu.VMEM((peers * CLIPS, BOTTLE), F32),
            pltpu.VMEM((peers * CLIPS, HS), F32),
            pltpu.VMEM((peers * CLIPS, block), F32),
        ],
    )
    return g_qkv, g_out.T, g_bottle


def solution(mesh):
    return program(mesh)


def program(mesh):
    return jax.shard_map(
        local,
        mesh=mesh,
        in_specs=(
            P("dp", "frame", "crop", None),
            P("dp", "crop", None),
            P(None, "frame"),
            P("frame", None),
            P(),
            P(None, "frame"),
            P("frame", None),
            P(),
            P(None, "frame"),
            P("frame"),
        ),
        out_specs=(P(("crop", "dp"), "frame"), P("frame", ("crop", "dp")), P(("crop", "dp"), None)),
        check_vma=False,
    )
```

```python
import functools
import math

import jax
import jax.numpy as jnp
from jax import lax
from jax.experimental import pallas as pl
from jax.experimental.pallas import tpu as pltpu
from jax.sharding import PartitionSpec as P


D = 1408
HS = 88
FRAMES = 16
BOTTLE = 256
GP = 8
ROWS = FRAMES * GP
TILES = 4
LFRAMES = 8
QKV = 3 * HS
PITCH = 272
CLIPS = 4
NTOK = 512
NTEACH = 4096
TAU_TEACH = 0.04
TAU_STUD = 0.1
ALL_CLIPS = 16
HIGH = lax.Precision.HIGHEST
F32 = jnp.float32
BF16 = jnp.bfloat16
NEG = -1e30
SCALE = 1.0 / math.sqrt(HS)
MSG = 24
QROWS = 56
STEP = 64.0
INTERPRET = False

NN = (((1,), (0,)), ((), ()))
NT = (((1,), (1,)), ((), ()))
TN = (((0,), (0,)), ((), ()))


def call(kernel, outs, *args, scratch=(), smem=0, hbm_in=(), hbm_out=(), any_in=(), limit=16):
    def space(index, in_hbm):
        if in_hbm is hbm_in and index in any_in:
            return pl.BlockSpec(memory_space=pl.ANY)
        return pl.BlockSpec(memory_space=pltpu.HBM if index in in_hbm else pltpu.VMEM)

    spec = [pl.BlockSpec(memory_space=pltpu.SMEM)] * smem
    spec += [space(index, hbm_in) for index in range(smem, len(args))]
    args = [pltpu.with_memory_space_constraint(arg, pltpu.HBM) if index in hbm_in else arg for index, arg in enumerate(args)]
    return pl.pallas_call(
        kernel,
        out_shape=tuple(
            pltpu.HBM(shape, dtype) if index in hbm_out else jax.ShapeDtypeStruct(shape, dtype)
            for index, (shape, dtype) in enumerate(outs)
        ),
        in_specs=spec,
        out_specs=tuple(space(index, hbm_out) for index in range(len(outs))),
        scratch_shapes=list(scratch),
        compiler_params=pltpu.CompilerParams(vmem_limit_bytes=limit * 2**20),
        interpret=INTERPRET,
    )(*args)


def room(*arrays):
    held = [pltpu.VMEM(tuple(array.shape), array.dtype) for array in arrays]
    return held + [pltpu.SemaphoreType.DMA((len(held),))]


def begin(sources, targets, sems):
    copies = [pltpu.make_async_copy(source, target, sems.at[i]) for i, (source, target) in enumerate(zip(sources, targets))]
    for copy in copies:
        copy.start()
    return copies


def mm(a, b, dims=NN):
    return lax.dot_general(a, b, dims, preferred_element_type=F32)


def mmh(a, b, dims=NN):
    return lax.dot_general(a, b, dims, precision=HIGH, preferred_element_type=F32)


def pieces(x):
    top = x.astype(BF16)
    rest = x - top.astype(F32)
    mid = rest.astype(BF16)
    return top, mid, (rest - mid.astype(F32)).astype(BF16)


def mm3(x, y, dims=NN):
    top, mid, low = pieces(x)
    return mm(top, y, dims) + (mm(mid, y, dims) + mm(low, y, dims))


def rsqrt(x):
    guess = lax.rsqrt(x)
    return guess * (1.5 - 0.5 * x * guess * guess)


def same_patch():
    row = lax.broadcasted_iota(jnp.int32, (ROWS, ROWS), 0)
    col = lax.broadcasted_iota(jnp.int32, (ROWS, ROWS), 1)
    return jnp.where((row % GP) == (col % GP), 0.0, NEG).astype(F32)


def split_qkv(flat, tile, head):
    rows = flat[tile * ROWS : (tile + 1) * ROWS]
    return [rows[:, head * PITCH + part * HS : head * PITCH + (part + 1) * HS].astype(BF16) for part in range(3)]


def spread_kernel(tok, out):
    half = out.shape[1]
    for peer in range(FRAMES):
        out[peer] = tok[(peer % 2) * half : (peer % 2 + 1) * half, :]


def prep_kernel(
    maps, frame, tok, t_out, t_oth, s_out, s_oth, t_bot, s_bot, mt, ms, otz, zlocal, plocal, ccol, crow
):
    total = jnp.sum(tok[...].astype(F32), axis=0, keepdims=True)
    otz[...] = mm3(total, t_bot[...])
    osz = mm3(total, s_bot[...])
    mt[0] = mm(t_out[...], t_bot[...])
    mt[1] = mm(t_oth[...], t_bot[...])
    ms[0] = mm(s_out[...], s_bot[...])
    ms[1] = mm(s_oth[...], s_bot[...])
    lane = lax.broadcasted_iota(jnp.int32, (1, ROWS), 1)
    row = lax.broadcasted_iota(jnp.int32, (ROWS, ROWS), 0) // GP
    down = [jnp.zeros((ROWS, ROWS), F32) for _ in range(CLIPS)]
    across = [jnp.zeros((1, ROWS), F32) for _ in range(CLIPS)]
    mine = [jnp.zeros((1, ROWS), F32) for _ in range(CLIPS)]
    for step in range(LFRAMES):
        for clip in range(CLIPS):
            index = maps[clip, step]
            down[clip] = down[clip] + jnp.where(row == index, 1.0, 0.0)
            across[clip] = across[clip] + jnp.where(lane // GP == index, 1.0, 0.0)
            mine[clip] = mine[clip] + jnp.where(index == frame[0], 1.0, 0.0)
    for clip in range(CLIPS):
        crow[clip] = down[clip]
        ccol[clip : clip + 1, :] = across[clip]
        frac = mine[clip][:, 0:1] / NTOK
        zlocal[clip : clip + 1, :] = frac * osz
        plocal[clip : clip + 1, :] = frac * total


def teacher_kernel(x, w_own_far, w_oth_far, mt_far, otz, normed, zt, weights, mt, sems):
    copies = begin((w_own_far, w_oth_far, mt_far), (weights.at[pl.ds(0, QKV)], weights.at[pl.ds(PITCH, QKV)], mt), sems)
    for group in range(2):
        values = x[:, group * 2 * GP : (group + 1) * 2 * GP, :].astype(F32)
        middle = jnp.mean(values, axis=-1, keepdims=True)
        moved = values - middle
        spread = jnp.mean(moved * moved, axis=-1, keepdims=True)
        token = moved * rsqrt(spread + 1e-06)
        normed[2 * group] = token[:, :GP].reshape(ROWS, D).astype(BF16)
        normed[2 * group + 1] = token[:, GP:].reshape(ROWS, D).astype(BF16)
    mask = same_patch()
    tokens = normed[...].reshape(TILES * ROWS, D)
    total = otz[...]
    for copy in copies:
        copy.wait()
    flat = mm(tokens, weights[...], NT)
    ones = jnp.ones((8, ROWS), BF16)
    for head in range(2):
        summed = jnp.zeros((8, HS), F32)
        for tile in range(TILES):
            query, key, value = split_qkv(flat, tile, head)
            scores = mm(key, query, NT) * SCALE + mask
            scores = jnp.exp(scores - jnp.max(scores, axis=0, keepdims=True))
            share = scores / jnp.sum(scores, axis=0, keepdims=True)
            received = mm(ones, share.astype(BF16), NT)
            summed = summed + mm3(received, value)
        total = total + mmh(summed[0:1], mt[head])
    for crop in range(zt.shape[0]):
        zt[crop] = total / NTEACH


def clip_shares(scores, count):
    here = jnp.where(count > 0.0, scores, NEG)
    here = jnp.exp(here - jnp.max(here, axis=0, keepdims=True))
    return here / jnp.sum(here * count, axis=0, keepdims=True)


def student_kernel(
    normed, w_own_far, w_oth_far, ms_far, s_out_far, s_oth_far, zlocal, plocal, ccol, crow,
    own_far, oth_far, shares_own_far, shares_oth_far, zs, pooled, heads,
    weights, ms, s_out, s_oth, sems, own, oth, shares_own, shares_oth, out_sems,
):
    copies = begin(
        (w_own_far, w_oth_far, ms_far, s_out_far, s_oth_far),
        (weights.at[pl.ds(0, QKV)], weights.at[pl.ds(PITCH, QKV)], ms, s_out, s_oth),
        sems,
    )
    mask = same_patch()
    tokens = normed[...].reshape(TILES * ROWS, D)
    leaving = []
    copies[0].wait()
    copies[1].wait()
    flat = mm(tokens, weights[...], NT)
    counts = jnp.concatenate([ccol[...], ccol[...]], axis=0).astype(BF16)
    sides = ((own, shares_own, own_far, shares_own_far), (oth, shares_oth, oth_far, shares_oth_far))
    for head, (keep, shares, keep_far, shares_far) in enumerate(sides):
        summed = jnp.zeros((CLIPS, HS), F32)
        for tile in range(TILES):
            query, key, value = split_qkv(flat, tile, head)
            keep[0, tile] = query
            keep[1, tile] = key
            keep[2, tile] = value
            scores = mm(key, query, NT) * SCALE + mask
            totals = []
            for clip in range(CLIPS):
                share = clip_shares(scores, crow[clip])
                shares[tile, clip, 0:ROWS, :] = share
                received = mm(counts, share.astype(BF16), NT)[clip : clip + 1]
                shares[tile, clip, ROWS : ROWS + 1, :] = received
                totals.append(received * ccol[clip : clip + 1, :])
            summed = summed + mm3(jnp.concatenate(totals, axis=0), value)
        leaving += begin((keep, shares), (keep_far, shares_far), out_sems.at[pl.ds(2 * head, 2)])
        heads[head] = summed / NTOK
    for copy in copies[2:]:
        copy.wait()
    zs[...] = mmh(heads[0], ms[0]) + mmh(heads[1], ms[1]) + zlocal[...]
    pooled[...] = mm3(heads[0], s_out[...]) + mm3(heads[1], s_oth[...]) + plocal[...]
    for copy in leaving:
        copy.wait()


def flip_kernel(normed, out_far, out, sems):
    out[...] = jnp.transpose(normed[...].reshape(TILES * ROWS, D))
    (copy,) = begin((out,), (out_far,), sems)
    copy.wait()


def message_kernel(frame, zs, ztc, pooled, heads, out):
    me = frame[0]
    zt = jnp.sum(ztc[...], axis=0)
    for peer in range(FRAMES):
        out[peer, 0:4, :] = zs[:, 0:128]
        out[peer, 4:8, :] = zs[:, 128:256]
        out[peer, 8:9, :] = zt[:, 0:128]
        out[peer, 9:10, :] = zt[:, 128:256]
        out[peer, 10:MSG, :] = jnp.zeros((MSG - 10, 128), F32)
        out[peer, 10:14, 0:HS] = pooled[:, peer * HS : (peer + 1) * HS]
        mine = (me == peer).astype(F32)
        partner = (jnp.bitwise_xor(me, 1) == peer).astype(F32)
        out[peer, 14:18, 0:HS] = heads[0] * mine + heads[1] * partner


def logits_kernel(got, protos, center, out, zs, heads):
    total = got[0]
    for source in range(1, FRAMES):
        total = total + got[source]
    z_s = jnp.concatenate([total[0:4], total[4:8]], axis=1)
    z_t = jnp.concatenate([total[8:9], total[9:10]], axis=1)
    zs[...] = z_s
    heads[...] = total[14:18, 0:HS]
    z_all = jnp.concatenate([z_s, z_t], axis=0)
    unit = z_all * rsqrt(jnp.sum(z_all * z_all, axis=-1, keepdims=True) + 1e-06)
    wide = mm3(unit, protos[...])
    logits = jnp.concatenate([wide[0:4] / TAU_STUD, (wide[4:5] - center[...]) / TAU_TEACH], axis=0)
    top = jnp.max(logits, axis=-1, keepdims=True)
    grown = jnp.exp(logits - top)
    size = jnp.sum(grown, axis=-1, keepdims=True)
    vec = mm3(grown, protos[...], NT)
    lane = lax.broadcasted_iota(jnp.int32, (5, 128), 1)
    tops = jnp.where(lane == 0, top, jnp.where(lane == 1, size, 0.0))
    for peer in range(FRAMES):
        out[peer, 0:5, :] = vec[:, 0:128]
        out[peer, 5:10, :] = vec[:, 128:256]
        out[peer, 10:15, :] = tops
        out[peer, 15:19, :] = total[10:14]
        out[peer, 19:MSG, :] = jnp.zeros((MSG - 19, 128), F32)


def code_of(peak):
    return jnp.ceil(jnp.log(jnp.maximum(peak, 1e-30)) * (STEP / math.log(2.0))) + 1.0


def scale_of(code):
    return jnp.exp(code * (math.log(2.0) / STEP))


def whole_max(x):
    return jnp.max(jnp.max(x, axis=-1, keepdims=True), axis=0, keepdims=True)


def stack2(parts):
    return jnp.concatenate([piece for part in parts for piece in pieces(part)[:2]], axis=0)


def back_kernel(
    peers, got, zs, heads, ms, own_far, oth_far, shares_own_far, shares_oth_far,
    ccol, crow, flip_own_far, flip_oth_far, out_far,
    keep_own, shares_own, keep_oth, shares_oth, flip, sems, out, out_sems, grad, rhs, last, line,
):
    count = TILES * ROWS
    copies = begin(
        (own_far, shares_own_far, oth_far, shares_oth_far, flip_own_far, flip_oth_far),
        (keep_own, shares_own, keep_oth, shares_oth, flip.at[:, pl.ds(0, count)], flip.at[:, pl.ds(count, count)]),
        sems,
    )
    tops = [got[source, 10:15, 0:1] for source in range(FRAMES)]
    top = functools.reduce(jnp.maximum, tops)
    size = jnp.zeros((5, 1), F32)
    low = jnp.zeros((5, 128), F32)
    high = jnp.zeros((5, 128), F32)
    for source in range(FRAMES):
        factor = jnp.exp(tops[source] - top)
        size = size + got[source, 10:15, 1:2] * factor
        low = low + got[source, 0:5, :] * factor
        high = high + got[source, 5:10, :] * factor
    expect = jnp.concatenate([low, high], axis=1) / size
    d_unit = (expect[0:4] - expect[4:5]) / (ALL_CLIPS * TAU_STUD)
    z_s = zs[...]
    inverse = rsqrt(jnp.sum(z_s * z_s, axis=-1, keepdims=True) + 1e-06)
    unit = z_s * inverse
    d_z = (d_unit - unit * jnp.sum(unit * d_unit, axis=-1, keepdims=True)) * inverse
    d_heads = mmh(d_z, ms[0], NT) / NTOK
    for half, (keep, shares) in enumerate(((keep_own, shares_own), (keep_oth, shares_oth))):
        copies[2 * half].wait()
        copies[2 * half + 1].wait()
        for tile in range(TILES):
            d_weights = mm3(d_heads, keep[2, tile], NT).astype(BF16).astype(F32)
            d_weights = d_weights * SCALE
            taken = [shares[tile, clip, ROWS : ROWS + 1, :] for clip in range(CLIPS)]
            d_down = jnp.transpose(jnp.concatenate([d_weights] + taken, axis=0))
            grow_q, grow_k = [], []
            for clip in range(CLIPS):
                count = ccol[clip : clip + 1, :]
                share = shares[tile, clip, 0:ROWS, :]
                d_w = jnp.broadcast_to(d_down[:, clip : clip + 1], (ROWS, ROWS))
                mean = jnp.sum(share * (crow[clip] * d_w), axis=0, keepdims=True)
                base = share * (d_w - mean)
                grow_k.append(base * count)
                grow_q.append(jnp.transpose(base) * count)
            wide_q = mm(stack2(grow_q), keep[1, tile])
            wide_k = mm(stack2(grow_k), keep[0, tile])
            totals = [jnp.zeros((ROWS, HS), F32) for _ in range(3)]
            for clip in range(CLIPS):
                many = crow[clip, :, 0:HS]
                first = 2 * clip * ROWS
                parts = [wide[first : first + ROWS] + wide[first + ROWS : first + 2 * ROWS] for wide in (wide_q, wide_k)]
                parts.append(d_down[:, CLIPS + clip : CLIPS + clip + 1] * d_heads[clip : clip + 1, :])
                totals = [total + many * part.astype(BF16).astype(F32) for total, part in zip(totals, parts)]
            packed = jnp.concatenate(totals, axis=1)
            first = packed.astype(BF16)
            second = (packed - first.astype(F32)).astype(BF16)
            rows = pl.ds((half * TILES + tile) * ROWS, ROWS)
            rhs[rows, 0:256] = first[:, 0:256]
            rhs[rows, 256:512] = second[:, 0:256]
            rhs[rows, 512:528] = jnp.concatenate([first[:, 256:264], second[:, 256:264]], axis=1)
    copies[4].wait()
    copies[5].wait()
    strip = D // 4
    thin = []
    for part in range(4):
        wide = mm(flip[part * strip : (part + 1) * strip, :], rhs[...])
        grad[part * strip : (part + 1) * strip, :] = wide[:, 0:256] + wide[:, 256:512]
        thin.append(wide[:, 512:520] + wide[:, 520:528])
    thin = jnp.transpose(jnp.concatenate(thin, axis=0))
    main = grad[...]
    code = code_of(jnp.max(jnp.abs(main), axis=0, keepdims=True))
    grad[...] = jnp.round(main * (32000.0 / scale_of(code)))
    code_thin = code_of(jnp.max(jnp.abs(thin), axis=-1, keepdims=True))
    last[...] = jnp.round(thin * (32000.0 / scale_of(code_thin)))
    code_z = code_of(whole_max(jnp.abs(d_z)))
    sent_z = jnp.round(d_z * (32000.0 / scale_of(code_z)))
    mine = heads[...]
    code_h = code_of(whole_max(jnp.abs(mine)))
    sent_h = jnp.round(mine * (32000.0 / scale_of(code_h)))
    pooled = jnp.concatenate([got[source, 15:19, 0:HS] for source in range(FRAMES)], axis=1)
    code_p = code_of(whole_max(jnp.abs(pooled)))
    sent_p = jnp.round(pooled * (32000.0 / scale_of(code_p)))
    lane = lax.broadcasted_iota(jnp.int32, (1, 128), 1)
    codes = jnp.where(lane == 64, code_z, jnp.where(lane == 65, code_h, jnp.where(lane == 66, code_p, 0.0)))
    block = D // peers
    line[...] = jnp.zeros((QROWS, 256), F32)
    line[44:48, :] = sent_z
    line[48:49, 0:HS] = sent_h[0:1]
    line[48:49, 128 : 128 + HS] = sent_h[1:2]
    line[49:50, 0:HS] = sent_h[2:3]
    line[49:50, 128 : 128 + HS] = sent_h[3:4]
    line[55:56, :] = code
    leaving = []
    for peer in range(peers):
        line[0:block, :] = grad[peer * block : (peer + 1) * block, :]
        part = sent_p[:, peer * block : (peer + 1) * block]
        line[50:54, 0:block] = part
        thin_part = last[:, peer * block : (peer + 1) * block]
        line[50:54, 64 : 64 + block] = thin_part[0:4]
        line[50:54, 128 : 128 + block] = thin_part[4:8]
        line[50:54, 192:193] = code_thin[0:4]
        line[50:54, 193:194] = code_thin[4:8]
        line[54:55, 0:128] = codes
        out[peer] = line[...].astype(jnp.int32).astype(jnp.int16)
        leaving += begin((out.at[peer],), (out_far.at[peer],), out_sems.at[pl.ds(peer, 1)])
    for copy in leaving:
        copy.wait()


def final_kernel(peers, got, bottle, g_qkv, g_out, g_bottle, z_all, h_all, p_all):
    block = D // peers
    main = jnp.zeros((block, 256), F32)
    thin_a = jnp.zeros((4, block), F32)
    thin_b = jnp.zeros((4, block), F32)
    for source in range(peers):
        line = got[source].astype(jnp.int32).astype(F32)
        main = main + line[0:block] * (scale_of(line[55:56]) / 32000.0)
        thin_a = thin_a + line[50:54, 64 : 64 + block] * (scale_of(line[50:54, 192:193]) / 32000.0)
        thin_b = thin_b + line[50:54, 128 : 128 + block] * (scale_of(line[50:54, 193:194]) / 32000.0)
        scales = scale_of(line[54:55, 0:128]) / 32000.0
        first = source * CLIPS
        z_all[first : first + 4, :] = line[44:48] * scales[:, 64:65]
        scale_h = scales[:, 65:66]
        h_all[first : first + 1, :] = line[48:49, 0:HS] * scale_h
        h_all[first + 1 : first + 2, :] = line[48:49, 128 : 128 + HS] * scale_h
        h_all[first + 2 : first + 3, :] = line[49:50, 0:HS] * scale_h
        h_all[first + 3 : first + 4, :] = line[49:50, 128 : 128 + HS] * scale_h
        p_all[first : first + 4, :] = line[50:54, 0:block] * scales[:, 66:67]
    g_qkv[:, 0:256] = main
    g_qkv[:, 256:264] = jnp.transpose(jnp.concatenate([thin_a, thin_b], axis=0))
    d_z = z_all[...]
    g_bottle[...] = mmh(p_all[...], d_z, TN)
    g_out[...] = mmh(bottle[...].astype(F32), mmh(h_all[...], d_z, TN), NT)


def local(
    global_clips,
    frame_map,
    teacher_qkv,
    teacher_out,
    teacher_bottle,
    student_qkv,
    student_out,
    student_bottle,
    prototypes,
    center,
):
    frame = lax.axis_index("frame")
    peers = lax.axis_size("crop") * lax.axis_size("dp")
    crops = lax.axis_size("crop")
    swap = [(index, index ^ 1) for index in range(FRAMES)]
    tokens = global_clips[0, 0]
    (spread,) = call(
        spread_kernel,
        [((FRAMES, tokens.shape[0] // 2, D), BF16)],
        tokens,
    )
    mixed = lax.all_to_all(spread, "frame", 0, 0, tiled=True)
    t_own = teacher_qkv.T
    s_own = student_qkv.T
    t_oth = lax.ppermute(t_own, "frame", swap)
    s_oth = lax.ppermute(s_own, "frame", swap)
    t_out_oth = lax.ppermute(teacher_out, "frame", swap)
    s_out_oth = lax.ppermute(student_out, "frame", swap)
    mt, ms, otz, zlocal, plocal, ccol, crow = call(
        prep_kernel,
        [
            ((2, HS, BOTTLE), F32),
            ((2, HS, BOTTLE), F32),
            ((1, BOTTLE), F32),
            ((CLIPS, BOTTLE), F32),
            ((CLIPS, D), F32),
            ((CLIPS, ROWS), F32),
            ((CLIPS, ROWS, ROWS), F32),
        ],
        frame_map[0], frame.astype(jnp.int32).reshape(1),
        tokens, teacher_out, t_out_oth, student_out, s_out_oth, teacher_bottle, student_bottle,
        smem=2,
    )
    normed, zt = call(
        teacher_kernel,
        [((TILES, ROWS, D), BF16), ((crops, 1, BOTTLE), F32)],
        mixed, t_own, t_oth, mt, otz,
        hbm_in=(1, 2, 3),
        scratch=[pltpu.VMEM((2 * PITCH, D), BF16), pltpu.VMEM(mt.shape, F32), pltpu.SemaphoreType.DMA((3,))],
    )
    ztc = lax.all_to_all(zt, "crop", 0, 0, tiled=True)
    keep = jax.ShapeDtypeStruct((3, TILES, ROWS, HS), BF16)
    table = jax.ShapeDtypeStruct((TILES, CLIPS, ROWS + 8, ROWS), F32)
    own, oth, shares_own, shares_oth, zs, pooled, heads = call(
        student_kernel,
        [
            (keep.shape, BF16),
            (keep.shape, BF16),
            (table.shape, F32),
            (table.shape, F32),
            ((CLIPS, BOTTLE), F32),
            ((CLIPS, D), F32),
            ((2, CLIPS, HS), F32),
        ],
        normed, s_own, s_oth, ms, student_out, s_out_oth, zlocal, plocal, ccol, crow,
        hbm_in=(1, 2, 3, 4, 5), hbm_out=(0, 1, 2, 3), limit=20,
        scratch=[pltpu.VMEM((2 * PITCH, D), BF16)]
        + room(ms, student_out, s_out_oth)[:-1]
        + [pltpu.SemaphoreType.DMA((5,))]
        + room(keep, keep, table, table),
    )
    (sent,) = call(
        message_kernel,
        [((FRAMES, MSG, 128), F32)],
        frame.astype(jnp.int32).reshape(1), zs, ztc, pooled, heads, smem=1,
    )
    sent, leaving = lax.optimization_barrier((sent, (normed, oth, shares_oth)))
    got = lax.all_to_all(sent, "frame", 0, 0, tiled=True)
    flat = jax.ShapeDtypeStruct((D, TILES * ROWS), BF16)
    (flipped,) = call(
        flip_kernel,
        [(flat.shape, BF16)],
        leaving[0],
        hbm_out=(0,), scratch=[pltpu.VMEM(flat.shape, BF16), pltpu.SemaphoreType.DMA((1,))],
    )
    flipped_oth = lax.ppermute(flipped, "frame", swap)
    shares_got = lax.ppermute(leaving[2], "frame", swap)
    kept_oth = lax.ppermute(leaving[1], "frame", swap)
    sent, z_s, my_heads = call(
        logits_kernel,
        [((FRAMES, MSG, 128), F32), ((CLIPS, BOTTLE), F32), ((CLIPS, HS), F32)],
        got, prototypes, center.reshape(1, -1),
    )
    got = lax.all_to_all(sent, "frame", 0, 0, tiled=True)
    (sent,) = call(
        functools.partial(back_kernel, peers),
        [((peers, QROWS, 256), jnp.int16)],
        got, z_s, my_heads, ms, own, kept_oth, shares_own, shares_got, ccol, crow, flipped, flipped_oth,
        hbm_in=(4, 6, 10, 11), any_in=(5, 7), hbm_out=(0,), limit=30,
        scratch=room(own, shares_own, kept_oth, shares_got)[:-1]
        + [
            pltpu.VMEM((D, 2 * TILES * ROWS), BF16),
            pltpu.SemaphoreType.DMA((6,)),
            pltpu.VMEM((peers, QROWS, 256), jnp.int16),
            pltpu.SemaphoreType.DMA((peers,)),
            pltpu.VMEM((D, 256), F32),
            pltpu.VMEM((2 * TILES * ROWS, 528), BF16),
            pltpu.VMEM((8, D), F32),
            pltpu.VMEM((QROWS, 256), F32),
        ],
    )
    got = lax.all_to_all(sent, ("crop", "dp"), 0, 0, tiled=True)
    block = D // peers
    place = lax.axis_index("crop") * lax.axis_size("dp") + lax.axis_index("dp")
    bottle = lax.dynamic_slice_in_dim(student_bottle, place * block, block, axis=0)
    g_qkv, g_out, g_bottle = call(
        functools.partial(final_kernel, peers),
        [((block, 3 * HS), F32), ((block, HS), F32), ((block, BOTTLE), F32)],
        got, bottle,
        scratch=[
            pltpu.VMEM((peers * CLIPS, BOTTLE), F32),
            pltpu.VMEM((peers * CLIPS, HS), F32),
            pltpu.VMEM((peers * CLIPS, block), F32),
        ],
    )
    return g_qkv, g_out.T, g_bottle


def solution(mesh):
    return program(mesh)


def program(mesh):
    return jax.shard_map(
        local,
        mesh=mesh,
        in_specs=(
            P("dp", "frame", "crop", None),
            P("dp", "crop", None),
            P(None, "frame"),
            P("frame", None),
            P(),
            P(None, "frame"),
            P("frame", None),
            P(),
            P(None, "frame"),
            P("frame"),
        ),
        out_specs=(P(("crop", "dp"), "frame"), P("frame", ("crop", "dp")), P(("crop", "dp"), None)),
        check_vma=False,
    )
```

```python
import functools
import math

import jax
import jax.numpy as jnp
from jax import lax
from jax.experimental import pallas as pl
from jax.experimental.pallas import tpu as pltpu
from jax.sharding import PartitionSpec as P


D = 1408
HS = 88
FRAMES = 16
BOTTLE = 256
GP = 8
ROWS = FRAMES * GP
TILES = 4
LFRAMES = 8
QKV = 3 * HS
PITCH = 272
CLIPS = 4
NTOK = 512
NTEACH = 4096
TAU_TEACH = 0.04
TAU_STUD = 0.1
ALL_CLIPS = 16
HIGH = lax.Precision.HIGHEST
F32 = jnp.float32
BF16 = jnp.bfloat16
NEG = -1e30
SCALE = 1.0 / math.sqrt(HS)
MSG = 24
QROWS = 56
STEP = 64.0
INTERPRET = False

NN = (((1,), (0,)), ((), ()))
NT = (((1,), (1,)), ((), ()))
TN = (((0,), (0,)), ((), ()))


def call(kernel, outs, *args, scratch=(), smem=0, hbm_in=(), hbm_out=(), any_in=(), limit=16):
    def space(index, in_hbm):
        if in_hbm is hbm_in and index in any_in:
            return pl.BlockSpec(memory_space=pl.ANY)
        return pl.BlockSpec(memory_space=pltpu.HBM if index in in_hbm else pltpu.VMEM)

    spec = [pl.BlockSpec(memory_space=pltpu.SMEM)] * smem
    spec += [space(index, hbm_in) for index in range(smem, len(args))]
    args = [pltpu.with_memory_space_constraint(arg, pltpu.HBM) if index in hbm_in else arg for index, arg in enumerate(args)]
    return pl.pallas_call(
        kernel,
        out_shape=tuple(
            pltpu.HBM(shape, dtype) if index in hbm_out else jax.ShapeDtypeStruct(shape, dtype)
            for index, (shape, dtype) in enumerate(outs)
        ),
        in_specs=spec,
        out_specs=tuple(space(index, hbm_out) for index in range(len(outs))),
        scratch_shapes=list(scratch),
        compiler_params=pltpu.CompilerParams(vmem_limit_bytes=limit * 2**20),
        interpret=INTERPRET,
    )(*args)


def room(*arrays):
    held = [pltpu.VMEM(tuple(array.shape), array.dtype) for array in arrays]
    return held + [pltpu.SemaphoreType.DMA((len(held),))]


def begin(sources, targets, sems):
    copies = [pltpu.make_async_copy(source, target, sems.at[i]) for i, (source, target) in enumerate(zip(sources, targets))]
    for copy in copies:
        copy.start()
    return copies


def mm(a, b, dims=NN):
    return lax.dot_general(a, b, dims, preferred_element_type=F32)


def mmh(a, b, dims=NN):
    return lax.dot_general(a, b, dims, precision=HIGH, preferred_element_type=F32)


def pieces(x):
    top = x.astype(BF16)
    rest = x - top.astype(F32)
    mid = rest.astype(BF16)
    return top, mid, (rest - mid.astype(F32)).astype(BF16)


def mm3(x, y, dims=NN):
    top, mid, low = pieces(x)
    return mm(top, y, dims) + (mm(mid, y, dims) + mm(low, y, dims))


def rsqrt(x):
    guess = lax.rsqrt(x)
    return guess * (1.5 - 0.5 * x * guess * guess)


def same_patch():
    row = lax.broadcasted_iota(jnp.int32, (ROWS, ROWS), 0)
    col = lax.broadcasted_iota(jnp.int32, (ROWS, ROWS), 1)
    return jnp.where((row % GP) == (col % GP), 0.0, NEG).astype(F32)


def split_qkv(flat, tile, head):
    rows = flat[tile * ROWS : (tile + 1) * ROWS]
    return [rows[:, head * PITCH + part * HS : head * PITCH + (part + 1) * HS].astype(BF16) for part in range(3)]


def spread_kernel(tok_far, out_far, tok, sems, out_sems):
    (copy,) = begin((tok_far,), (tok,), sems)
    copy.wait()
    half = out_far.shape[1]
    leaving = begin(
        [tok.at[pl.ds((peer % 2) * half, half)] for peer in range(FRAMES)],
        [out_far.at[peer] for peer in range(FRAMES)],
        out_sems,
    )
    for copy in leaving:
        copy.wait()


def prep_kernel(
    maps, frame, tok, t_out, t_oth, s_out, s_oth, t_bot, s_bot, mt, ms, otz, zlocal, plocal, ccol, crow
):
    total = jnp.sum(tok[...].astype(F32), axis=0, keepdims=True)
    otz[...] = mm3(total, t_bot[...])
    osz = mm3(total, s_bot[...])
    mt[0] = mm(t_out[...], t_bot[...])
    mt[1] = mm(t_oth[...], t_bot[...])
    ms[0] = mm(s_out[...], s_bot[...])
    ms[1] = mm(s_oth[...], s_bot[...])
    lane = lax.broadcasted_iota(jnp.int32, (1, ROWS), 1)
    row = lax.broadcasted_iota(jnp.int32, (ROWS, ROWS), 0) // GP
    down = [jnp.zeros((ROWS, ROWS), F32) for _ in range(CLIPS)]
    across = [jnp.zeros((1, ROWS), F32) for _ in range(CLIPS)]
    mine = [jnp.zeros((1, ROWS), F32) for _ in range(CLIPS)]
    for step in range(LFRAMES):
        for clip in range(CLIPS):
            index = maps[clip, step]
            down[clip] = down[clip] + jnp.where(row == index, 1.0, 0.0)
            across[clip] = across[clip] + jnp.where(lane // GP == index, 1.0, 0.0)
            mine[clip] = mine[clip] + jnp.where(index == frame[0], 1.0, 0.0)
    for clip in range(CLIPS):
        crow[clip] = down[clip]
        ccol[clip : clip + 1, :] = across[clip]
        frac = mine[clip][:, 0:1] / NTOK
        zlocal[clip : clip + 1, :] = frac * osz
        plocal[clip : clip + 1, :] = frac * total


def teacher_kernel(x, w_own_far, w_oth_far, mt_far, otz, normed, zt, weights, mt, sems):
    copies = begin((w_own_far, w_oth_far, mt_far), (weights.at[pl.ds(0, QKV)], weights.at[pl.ds(PITCH, QKV)], mt), sems)
    for group in range(2):
        values = x[:, group * 2 * GP : (group + 1) * 2 * GP, :].astype(F32)
        middle = jnp.mean(values, axis=-1, keepdims=True)
        moved = values - middle
        spread = jnp.mean(moved * moved, axis=-1, keepdims=True)
        token = moved * rsqrt(spread + 1e-06)
        normed[2 * group] = token[:, :GP].reshape(ROWS, D).astype(BF16)
        normed[2 * group + 1] = token[:, GP:].reshape(ROWS, D).astype(BF16)
    mask = same_patch()
    tokens = normed[...].reshape(TILES * ROWS, D)
    total = otz[...]
    for copy in copies:
        copy.wait()
    flat = mm(tokens, weights[...], NT)
    ones = jnp.ones((8, ROWS), BF16)
    for head in range(2):
        summed = jnp.zeros((8, HS), F32)
        for tile in range(TILES):
            query, key, value = split_qkv(flat, tile, head)
            scores = mm(key, query, NT) * SCALE + mask
            scores = jnp.exp(scores - jnp.max(scores, axis=0, keepdims=True))
            share = scores / jnp.sum(scores, axis=0, keepdims=True)
            received = mm(ones, share.astype(BF16), NT)
            summed = summed + mm3(received, value)
        total = total + mmh(summed[0:1], mt[head])
    for crop in range(zt.shape[0]):
        zt[crop] = total / NTEACH


def clip_shares(scores, count):
    here = jnp.where(count > 0.0, scores, NEG)
    here = jnp.exp(here - jnp.max(here, axis=0, keepdims=True))
    return here / jnp.sum(here * count, axis=0, keepdims=True)


def student_kernel(
    normed, w_own_far, w_oth_far, ms_far, s_out_far, s_oth_far, zlocal, plocal, ccol, crow,
    own_far, oth_far, shares_own_far, shares_oth_far, zs, pooled, heads,
    weights, ms, s_out, s_oth, sems, own, oth, shares_own, shares_oth, out_sems,
):
    copies = begin(
        (w_own_far, w_oth_far, ms_far, s_out_far, s_oth_far),
        (weights.at[pl.ds(0, QKV)], weights.at[pl.ds(PITCH, QKV)], ms, s_out, s_oth),
        sems,
    )
    mask = same_patch()
    tokens = normed[...].reshape(TILES * ROWS, D)
    leaving = []
    copies[0].wait()
    copies[1].wait()
    flat = mm(tokens, weights[...], NT)
    counts = jnp.concatenate([ccol[...], ccol[...]], axis=0).astype(BF16)
    sides = ((own, shares_own, own_far, shares_own_far), (oth, shares_oth, oth_far, shares_oth_far))
    for head, (keep, shares, keep_far, shares_far) in enumerate(sides):
        summed = jnp.zeros((CLIPS, HS), F32)
        for tile in range(TILES):
            query, key, value = split_qkv(flat, tile, head)
            keep[0, tile] = query
            keep[1, tile] = key
            keep[2, tile] = value
            scores = mm(key, query, NT) * SCALE + mask
            totals = []
            for clip in range(CLIPS):
                share = clip_shares(scores, crow[clip])
                shares[tile, clip, 0:ROWS, :] = share
                received = mm(counts, share.astype(BF16), NT)[clip : clip + 1]
                shares[tile, clip, ROWS : ROWS + 1, :] = received
                totals.append(received * ccol[clip : clip + 1, :])
            summed = summed + mm3(jnp.concatenate(totals, axis=0), value)
        leaving += begin((keep, shares), (keep_far, shares_far), out_sems.at[pl.ds(2 * head, 2)])
        heads[head] = summed / NTOK
    for copy in copies[2:]:
        copy.wait()
    zs[...] = mmh(heads[0], ms[0]) + mmh(heads[1], ms[1]) + zlocal[...]
    pooled[...] = mm3(heads[0], s_out[...]) + mm3(heads[1], s_oth[...]) + plocal[...]
    for copy in leaving:
        copy.wait()


def flip_kernel(normed, out_far, out, sems):
    out[...] = jnp.transpose(normed[...].reshape(TILES * ROWS, D))
    (copy,) = begin((out,), (out_far,), sems)
    copy.wait()


def message_kernel(frame, zs, ztc, pooled, heads, out):
    me = frame[0]
    zt = jnp.sum(ztc[...], axis=0)
    for peer in range(FRAMES):
        out[peer, 0:4, :] = zs[:, 0:128]
        out[peer, 4:8, :] = zs[:, 128:256]
        out[peer, 8:9, :] = zt[:, 0:128]
        out[peer, 9:10, :] = zt[:, 128:256]
        out[peer, 10:MSG, :] = jnp.zeros((MSG - 10, 128), F32)
        out[peer, 10:14, 0:HS] = pooled[:, peer * HS : (peer + 1) * HS]
        mine = (me == peer).astype(F32)
        partner = (jnp.bitwise_xor(me, 1) == peer).astype(F32)
        out[peer, 14:18, 0:HS] = heads[0] * mine + heads[1] * partner


def logits_kernel(got, protos, center, out, zs, heads):
    total = got[0]
    for source in range(1, FRAMES):
        total = total + got[source]
    z_s = jnp.concatenate([total[0:4], total[4:8]], axis=1)
    z_t = jnp.concatenate([total[8:9], total[9:10]], axis=1)
    zs[...] = z_s
    heads[...] = total[14:18, 0:HS]
    z_all = jnp.concatenate([z_s, z_t], axis=0)
    unit = z_all * rsqrt(jnp.sum(z_all * z_all, axis=-1, keepdims=True) + 1e-06)
    wide = mm3(unit, protos[...])
    logits = jnp.concatenate([wide[0:4] / TAU_STUD, (wide[4:5] - center[...]) / TAU_TEACH], axis=0)
    top = jnp.max(logits, axis=-1, keepdims=True)
    grown = jnp.exp(logits - top)
    size = jnp.sum(grown, axis=-1, keepdims=True)
    vec = mm3(grown, protos[...], NT)
    lane = lax.broadcasted_iota(jnp.int32, (5, 128), 1)
    tops = jnp.where(lane == 0, top, jnp.where(lane == 1, size, 0.0))
    for peer in range(FRAMES):
        out[peer, 0:5, :] = vec[:, 0:128]
        out[peer, 5:10, :] = vec[:, 128:256]
        out[peer, 10:15, :] = tops
        out[peer, 15:19, :] = total[10:14]
        out[peer, 19:MSG, :] = jnp.zeros((MSG - 19, 128), F32)


def code_of(peak):
    return jnp.ceil(jnp.log(jnp.maximum(peak, 1e-30)) * (STEP / math.log(2.0))) + 1.0


def scale_of(code):
    return jnp.exp(code * (math.log(2.0) / STEP))


def whole_max(x):
    return jnp.max(jnp.max(x, axis=-1, keepdims=True), axis=0, keepdims=True)


def stack2(parts):
    return jnp.concatenate([piece for part in parts for piece in pieces(part)[:2]], axis=0)


def back_kernel(
    peers, got, zs, heads, ms, own_far, oth_far, shares_own_far, shares_oth_far,
    ccol, crow, flip_own_far, flip_oth_far, out_far,
    keep_own, shares_own, keep_oth, shares_oth, flip, sems, out, out_sems, grad, rhs, last, line,
):
    count = TILES * ROWS
    copies = begin(
        (own_far, shares_own_far, oth_far, shares_oth_far, flip_own_far, flip_oth_far),
        (keep_own, shares_own, keep_oth, shares_oth, flip.at[:, pl.ds(0, count)], flip.at[:, pl.ds(count, count)]),
        sems,
    )
    tops = [got[source, 10:15, 0:1] for source in range(FRAMES)]
    top = functools.reduce(jnp.maximum, tops)
    size = jnp.zeros((5, 1), F32)
    low = jnp.zeros((5, 128), F32)
    high = jnp.zeros((5, 128), F32)
    for source in range(FRAMES):
        factor = jnp.exp(tops[source] - top)
        size = size + got[source, 10:15, 1:2] * factor
        low = low + got[source, 0:5, :] * factor
        high = high + got[source, 5:10, :] * factor
    expect = jnp.concatenate([low, high], axis=1) / size
    d_unit = (expect[0:4] - expect[4:5]) / (ALL_CLIPS * TAU_STUD)
    z_s = zs[...]
    inverse = rsqrt(jnp.sum(z_s * z_s, axis=-1, keepdims=True) + 1e-06)
    unit = z_s * inverse
    d_z = (d_unit - unit * jnp.sum(unit * d_unit, axis=-1, keepdims=True)) * inverse
    d_heads = mmh(d_z, ms[0], NT) / NTOK
    for half, (keep, shares) in enumerate(((keep_own, shares_own), (keep_oth, shares_oth))):
        copies[2 * half].wait()
        copies[2 * half + 1].wait()
        for tile in range(TILES):
            d_weights = mm3(d_heads, keep[2, tile], NT).astype(BF16).astype(F32)
            d_weights = d_weights * SCALE
            taken = [shares[tile, clip, ROWS : ROWS + 1, :] for clip in range(CLIPS)]
            d_down = jnp.transpose(jnp.concatenate([d_weights] + taken, axis=0))
            grow_q, grow_k = [], []
            for clip in range(CLIPS):
                count = ccol[clip : clip + 1, :]
                share = shares[tile, clip, 0:ROWS, :]
                d_w = jnp.broadcast_to(d_down[:, clip : clip + 1], (ROWS, ROWS))
                mean = jnp.sum(share * (crow[clip] * d_w), axis=0, keepdims=True)
                base = share * (d_w - mean)
                grow_k.append(base * count)
                grow_q.append(jnp.transpose(base) * count)
            wide_q = mm(stack2(grow_q), keep[1, tile])
            wide_k = mm(stack2(grow_k), keep[0, tile])
            totals = [jnp.zeros((ROWS, HS), F32) for _ in range(3)]
            for clip in range(CLIPS):
                many = crow[clip, :, 0:HS]
                first = 2 * clip * ROWS
                parts = [wide[first : first + ROWS] + wide[first + ROWS : first + 2 * ROWS] for wide in (wide_q, wide_k)]
                parts.append(d_down[:, CLIPS + clip : CLIPS + clip + 1] * d_heads[clip : clip + 1, :])
                totals = [total + many * part.astype(BF16).astype(F32) for total, part in zip(totals, parts)]
            packed = jnp.concatenate(totals, axis=1)
            first = packed.astype(BF16)
            second = (packed - first.astype(F32)).astype(BF16)
            rows = pl.ds((half * TILES + tile) * ROWS, ROWS)
            rhs[rows, 0:256] = first[:, 0:256]
            rhs[rows, 256:512] = second[:, 0:256]
            rhs[rows, 512:528] = jnp.concatenate([first[:, 256:264], second[:, 256:264]], axis=1)
    copies[4].wait()
    copies[5].wait()
    strip = D // 4
    thin = []
    for part in range(4):
        wide = mm(flip[part * strip : (part + 1) * strip, :], rhs[...])
        grad[part * strip : (part + 1) * strip, :] = wide[:, 0:256] + wide[:, 256:512]
        thin.append(wide[:, 512:520] + wide[:, 520:528])
    thin = jnp.transpose(jnp.concatenate(thin, axis=0))
    main = grad[...]
    code = code_of(jnp.max(jnp.abs(main), axis=0, keepdims=True))
    grad[...] = jnp.round(main * (32000.0 / scale_of(code)))
    code_thin = code_of(jnp.max(jnp.abs(thin), axis=-1, keepdims=True))
    last[...] = jnp.round(thin * (32000.0 / scale_of(code_thin)))
    code_z = code_of(whole_max(jnp.abs(d_z)))
    sent_z = jnp.round(d_z * (32000.0 / scale_of(code_z)))
    mine = heads[...]
    code_h = code_of(whole_max(jnp.abs(mine)))
    sent_h = jnp.round(mine * (32000.0 / scale_of(code_h)))
    pooled = jnp.concatenate([got[source, 15:19, 0:HS] for source in range(FRAMES)], axis=1)
    code_p = code_of(whole_max(jnp.abs(pooled)))
    sent_p = jnp.round(pooled * (32000.0 / scale_of(code_p)))
    lane = lax.broadcasted_iota(jnp.int32, (1, 128), 1)
    codes = jnp.where(lane == 64, code_z, jnp.where(lane == 65, code_h, jnp.where(lane == 66, code_p, 0.0)))
    block = D // peers
    line[...] = jnp.zeros((QROWS, 256), F32)
    line[44:48, :] = sent_z
    line[48:49, 0:HS] = sent_h[0:1]
    line[48:49, 128 : 128 + HS] = sent_h[1:2]
    line[49:50, 0:HS] = sent_h[2:3]
    line[49:50, 128 : 128 + HS] = sent_h[3:4]
    line[55:56, :] = code
    leaving = []
    for peer in range(peers):
        line[0:block, :] = grad[peer * block : (peer + 1) * block, :]
        part = sent_p[:, peer * block : (peer + 1) * block]
        line[50:54, 0:block] = part
        thin_part = last[:, peer * block : (peer + 1) * block]
        line[50:54, 64 : 64 + block] = thin_part[0:4]
        line[50:54, 128 : 128 + block] = thin_part[4:8]
        line[50:54, 192:193] = code_thin[0:4]
        line[50:54, 193:194] = code_thin[4:8]
        line[54:55, 0:128] = codes
        out[peer] = line[...].astype(jnp.int32).astype(jnp.int16)
        leaving += begin((out.at[peer],), (out_far.at[peer],), out_sems.at[pl.ds(peer, 1)])
    for copy in leaving:
        copy.wait()


def final_kernel(peers, got, bottle, g_qkv, g_out, g_bottle, z_all, h_all, p_all):
    block = D // peers
    main = jnp.zeros((block, 256), F32)
    thin_a = jnp.zeros((4, block), F32)
    thin_b = jnp.zeros((4, block), F32)
    for source in range(peers):
        line = got[source].astype(jnp.int32).astype(F32)
        main = main + line[0:block] * (scale_of(line[55:56]) / 32000.0)
        thin_a = thin_a + line[50:54, 64 : 64 + block] * (scale_of(line[50:54, 192:193]) / 32000.0)
        thin_b = thin_b + line[50:54, 128 : 128 + block] * (scale_of(line[50:54, 193:194]) / 32000.0)
        scales = scale_of(line[54:55, 0:128]) / 32000.0
        first = source * CLIPS
        z_all[first : first + 4, :] = line[44:48] * scales[:, 64:65]
        scale_h = scales[:, 65:66]
        h_all[first : first + 1, :] = line[48:49, 0:HS] * scale_h
        h_all[first + 1 : first + 2, :] = line[48:49, 128 : 128 + HS] * scale_h
        h_all[first + 2 : first + 3, :] = line[49:50, 0:HS] * scale_h
        h_all[first + 3 : first + 4, :] = line[49:50, 128 : 128 + HS] * scale_h
        p_all[first : first + 4, :] = line[50:54, 0:block] * scales[:, 66:67]
    g_qkv[:, 0:256] = main
    g_qkv[:, 256:264] = jnp.transpose(jnp.concatenate([thin_a, thin_b], axis=0))
    d_z = z_all[...]
    g_bottle[...] = mmh(p_all[...], d_z, TN)
    g_out[...] = mmh(bottle[...].astype(F32), mmh(h_all[...], d_z, TN), NT)


def local(
    global_clips,
    frame_map,
    teacher_qkv,
    teacher_out,
    teacher_bottle,
    student_qkv,
    student_out,
    student_bottle,
    prototypes,
    center,
):
    frame = lax.axis_index("frame")
    peers = lax.axis_size("crop") * lax.axis_size("dp")
    crops = lax.axis_size("crop")
    swap = [(index, index ^ 1) for index in range(FRAMES)]
    tokens = global_clips[0, 0]
    (spread,) = call(
        spread_kernel,
        [((FRAMES, tokens.shape[0] // 2, D), BF16)],
        tokens,
        hbm_in=(0,), hbm_out=(0,), scratch=room(tokens) + [pltpu.SemaphoreType.DMA((FRAMES,))],
    )
    mixed = lax.all_to_all(spread, "frame", 0, 0, tiled=True)
    t_own = teacher_qkv.T
    s_own = student_qkv.T
    t_oth = lax.ppermute(t_own, "frame", swap)
    s_oth = lax.ppermute(s_own, "frame", swap)
    t_out_oth = lax.ppermute(teacher_out, "frame", swap)
    s_out_oth = lax.ppermute(student_out, "frame", swap)
    mt, ms, otz, zlocal, plocal, ccol, crow = call(
        prep_kernel,
        [
            ((2, HS, BOTTLE), F32),
            ((2, HS, BOTTLE), F32),
            ((1, BOTTLE), F32),
            ((CLIPS, BOTTLE), F32),
            ((CLIPS, D), F32),
            ((CLIPS, ROWS), F32),
            ((CLIPS, ROWS, ROWS), F32),
        ],
        frame_map[0], frame.astype(jnp.int32).reshape(1),
        tokens, teacher_out, t_out_oth, student_out, s_out_oth, teacher_bottle, student_bottle,
        smem=2,
    )
    normed, zt = call(
        teacher_kernel,
        [((TILES, ROWS, D), BF16), ((crops, 1, BOTTLE), F32)],
        mixed, t_own, t_oth, mt, otz,
        hbm_in=(1, 2, 3),
        scratch=[pltpu.VMEM((2 * PITCH, D), BF16), pltpu.VMEM(mt.shape, F32), pltpu.SemaphoreType.DMA((3,))],
    )
    ztc = lax.all_to_all(zt, "crop", 0, 0, tiled=True)
    keep = jax.ShapeDtypeStruct((3, TILES, ROWS, HS), BF16)
    table = jax.ShapeDtypeStruct((TILES, CLIPS, ROWS + 8, ROWS), F32)
    own, oth, shares_own, shares_oth, zs, pooled, heads = call(
        student_kernel,
        [
            (keep.shape, BF16),
            (keep.shape, BF16),
            (table.shape, F32),
            (table.shape, F32),
            ((CLIPS, BOTTLE), F32),
            ((CLIPS, D), F32),
            ((2, CLIPS, HS), F32),
        ],
        normed, s_own, s_oth, ms, student_out, s_out_oth, zlocal, plocal, ccol, crow,
        hbm_in=(1, 2, 3, 4, 5), hbm_out=(0, 1, 2, 3), limit=20,
        scratch=[pltpu.VMEM((2 * PITCH, D), BF16)]
        + room(ms, student_out, s_out_oth)[:-1]
        + [pltpu.SemaphoreType.DMA((5,))]
        + room(keep, keep, table, table),
    )
    (sent,) = call(
        message_kernel,
        [((FRAMES, MSG, 128), F32)],
        frame.astype(jnp.int32).reshape(1), zs, ztc, pooled, heads, smem=1,
    )
    sent, leaving = lax.optimization_barrier((sent, (normed, oth, shares_oth)))
    got = lax.all_to_all(sent, "frame", 0, 0, tiled=True)
    flat = jax.ShapeDtypeStruct((D, TILES * ROWS), BF16)
    (flipped,) = call(
        flip_kernel,
        [(flat.shape, BF16)],
        leaving[0],
        hbm_out=(0,), scratch=[pltpu.VMEM(flat.shape, BF16), pltpu.SemaphoreType.DMA((1,))],
    )
    flipped_oth = lax.ppermute(flipped, "frame", swap)
    shares_got = lax.ppermute(leaving[2], "frame", swap)
    kept_oth = lax.ppermute(leaving[1], "frame", swap)
    sent, z_s, my_heads = call(
        logits_kernel,
        [((FRAMES, MSG, 128), F32), ((CLIPS, BOTTLE), F32), ((CLIPS, HS), F32)],
        got, prototypes, center.reshape(1, -1),
    )
    got = lax.all_to_all(sent, "frame", 0, 0, tiled=True)
    (sent,) = call(
        functools.partial(back_kernel, peers),
        [((peers, QROWS, 256), jnp.int16)],
        got, z_s, my_heads, ms, own, kept_oth, shares_own, shares_got, ccol, crow, flipped, flipped_oth,
        hbm_in=(4, 6, 10, 11), any_in=(5, 7), hbm_out=(0,), limit=30,
        scratch=room(own, shares_own, kept_oth, shares_got)[:-1]
        + [
            pltpu.VMEM((D, 2 * TILES * ROWS), BF16),
            pltpu.SemaphoreType.DMA((6,)),
            pltpu.VMEM((peers, QROWS, 256), jnp.int16),
            pltpu.SemaphoreType.DMA((peers,)),
            pltpu.VMEM((D, 256), F32),
            pltpu.VMEM((2 * TILES * ROWS, 528), BF16),
            pltpu.VMEM((8, D), F32),
            pltpu.VMEM((QROWS, 256), F32),
        ],
    )
    got = lax.all_to_all(sent, ("crop", "dp"), 0, 0, tiled=True)
    block = D // peers
    place = lax.axis_index("crop") * lax.axis_size("dp") + lax.axis_index("dp")
    bottle = lax.dynamic_slice_in_dim(student_bottle, place * block, block, axis=0)
    g_qkv, g_out, g_bottle = call(
        functools.partial(final_kernel, peers),
        [((block, 3 * HS), F32), ((block, HS), F32), ((block, BOTTLE), F32)],
        got, bottle,
        scratch=[
            pltpu.VMEM((peers * CLIPS, BOTTLE), F32),
            pltpu.VMEM((peers * CLIPS, HS), F32),
            pltpu.VMEM((peers * CLIPS, block), F32),
        ],
    )
    return g_qkv, g_out.T, g_bottle


def solution(mesh):
    return program(mesh)


def program(mesh):
    return jax.shard_map(
        local,
        mesh=mesh,
        in_specs=(
            P("dp", "frame", "crop", None),
            P("dp", "crop", None),
            P(None, "frame"),
            P("frame", None),
            P(),
            P(None, "frame"),
            P("frame", None),
            P(),
            P(None, "frame"),
            P("frame"),
        ),
        out_specs=(P(("crop", "dp"), "frame"), P("frame", ("crop", "dp")), P(("crop", "dp"), None)),
        check_vma=False,
    )
```
